32 devices in a mesh: row: 8 (over z, x), col: 4 (over y, core).
Axes of the slice: x: 2, y: 2, z: 4, core: 2. Of those that a mesh axis runs over, the one named last changes fastest.
Arguments:
- pixels: bfloat16 [512, 512, 384], P('row', 'col'), may hold values from -40 to 40, as said below
- start: float32 [384, 64], replicated, may hold values from -0.3125 to 0.3125
Outputs:
- mean: float32 [384], replicated
- projector: float32 [384, 384], replicated
- scores: float32 [64, 512, 512], P(None, 'row', 'col')
The draws below stay inside these ranges and needn't reach their ends.
Inputs may be any that keep to these rules, and one draw needn't show every extreme that they name: `pixels`: Real-valued features.
All inputs are finite; a program needn't handle non-finite values.
Results may differ from the reference program's by a relative error of at most 0.0029.
Values may be sent and summed in bfloat16 or wider, within the bound.
No kernel may reach another device: no remote copies, remote signals or barrier semaphores. Data moves between devices by JAX's collectives and lax.ppermute only.
A program may use at most 64 MiB of HBM per device.

```python
import jax
import jax.numpy as jnp
from jax import lax

FEAT = 384
RANK = 64
ITERS = 4
TILE_ROWS = 64
ROWS = 512
COLS = 512


def draw_pixels(key, part):
    base_key = jax.random.fold_in(key, 17)
    keys = jax.random.split(base_key, 7)
    order = jnp.arange(FEAT, dtype=jnp.float32) + 1.0
    decay = order ** (-0.5)
    spread = jnp.exp(jax.random.uniform(keys[0], (FEAT,), jnp.float32, jnp.log(0.3), jnp.log(1.0)))
    level = jnp.clip(0.7 * jax.random.normal(keys[1], (FEAT,), jnp.float32), -2.8, 2.8)
    mixing = jnp.clip(jax.random.normal(keys[2], (FEAT, FEAT), jnp.float32), -4.0, 4.0)
    factor = 1.4 / jnp.sqrt(jnp.sum(decay * decay))
    mixing = mixing * (decay * factor)[:, None]
    row_freq = jax.random.uniform(keys[3], (FEAT,), jnp.float32, 0.5, 6.0)
    col_freq = jax.random.uniform(keys[4], (FEAT,), jnp.float32, -6.0, 6.0)
    phase = jax.random.uniform(keys[5], (FEAT,), jnp.float32, 0.0, 6.2831853)
    across = jnp.arange(COLS, dtype=jnp.float32)
    across_trend = 1.0 + across / max(COLS - 1, 1)
    block_key = keys[6]

    def one_block(index):
        rough_key, noise_key = jax.random.split(jax.random.fold_in(block_key, index), 2)
        position = (index * TILE_ROWS + jnp.arange(TILE_ROWS, dtype=jnp.int32)).astype(jnp.float32)
        angle = 6.2831853 * (position[:, None, None] / ROWS * row_freq + across[None, :, None] / COLS * col_freq) + phase
        rough = jnp.clip(jax.random.normal(rough_key, (TILE_ROWS, COLS, FEAT), jnp.float32), -4.0, 4.0)
        noise = jnp.clip(jax.random.normal(noise_key, (TILE_ROWS, COLS, FEAT), jnp.float32), -4.0, 4.0)
        latent = 1.4142135 * jnp.cos(angle) + rough
        mixed = jnp.dot(latent.reshape(TILE_ROWS * COLS, FEAT), mixing, precision=lax.Precision.HIGHEST)
        mixed = mixed.reshape(TILE_ROWS, COLS, FEAT)
        trend = (1.0 + 2.0 * position / max(ROWS - 1, 1))[:, None] * across_trend[None, :]
        return mixed + spread * noise + level * trend[:, :, None]
    blocks = lax.map(one_block, jnp.arange(ROWS // TILE_ROWS, dtype=jnp.int32))
    return jnp.clip(blocks.reshape(ROWS, COLS, FEAT), -40.0, 40.0).astype(jnp.bfloat16)


def bell_draw(own_key, dims, deviation, bound, held_as=jnp.bfloat16):
    result = deviation * jax.random.normal(own_key, dims, jnp.float32)
    return jnp.clip(result, min=-bound, max=bound).astype(held_as)


def setup_inputs(seed: int = 0) -> dict:
    arg_keys = jax.random.split(jax.random.key(seed), 3)
    pixels = draw_pixels(jax.random.fold_in(arg_keys[2], 71), 0)
    start = bell_draw(arg_keys[1], (FEAT, RANK), FEAT ** -0.5, 0.3125, jnp.float32)
    return {"pixels": pixels, "start": start}


GAUSS = (0.0625, 0.25, 0.375, 0.25, 0.0625)

def edge_weight(first, count, total):
    position = first + jnp.arange(count, dtype=jnp.int32)
    weight = jnp.zeros((count,), jnp.float32)
    for offset in range(5):
        inside = (position + offset - 2 >= 0) & (position + offset - 2 < total)
        weight = weight + GAUSS[offset] * inside.astype(jnp.float32)
    return weight

def along_rows(padded, count):
    total = GAUSS[0] * padded[0:count].astype(jnp.float32)
    for offset in range(1, 5):
        total = total + GAUSS[offset] * padded[offset:offset + count].astype(jnp.float32)
    return total

def along_cols(padded, count):
    total = GAUSS[0] * padded[:, 0:count].astype(jnp.float32)
    for offset in range(1, 5):
        total = total + GAUSS[offset] * padded[:, offset:offset + count].astype(jnp.float32)
    return total

def orthonormal(product):
    inner = jnp.dot(product.T, product, precision=lax.Precision.HIGHEST)
    lower_factor = jnp.linalg.cholesky(inner)
    return lax.linalg.triangular_solve(lower_factor, product, left_side=False, lower=True, transpose_a=True)

def reference(pixels, start):
    width = 64 if FEAT % 64 == 0 else FEAT
    weight = edge_weight(0, ROWS, ROWS)[:, None, None] * edge_weight(0, COLS, COLS)[None, :, None]
    pieces = []
    for first in range(0, FEAT, width):
        part = pixels[:, :, first:first + width]
        padded = jnp.pad(part, ((2, 2), (2, 2), (0, 0)))
        blurred = along_cols(along_rows(padded, ROWS), COLS)
        pieces.append((blurred / weight).astype(jnp.bfloat16))
    smoothed = jnp.concatenate(pieces, axis=2)
    flat = smoothed.reshape(ROWS * COLS, FEAT)
    gram = lax.dot_general(flat.astype(jnp.float32), flat.astype(jnp.float32), (((0,), (0,)), ((), ())), preferred_element_type=jnp.float32)
    sums = jnp.sum(flat, axis=0, dtype=jnp.float32)
    count = float(ROWS * COLS)
    mean = sums / count
    cov = gram / count - mean[:, None] * mean[None, :]
    basis = start
    for step in range(ITERS):
        basis = orthonormal(jnp.dot(cov, basis, precision=lax.Precision.HIGHEST))
    projector = jnp.dot(basis, basis.T, precision=lax.Precision.HIGHEST)
    basis_b = basis.astype(jnp.bfloat16)
    shift = jnp.dot(mean, basis_b.astype(jnp.float32), precision=lax.Precision.HIGHEST)
    scores = lax.dot_general(basis_b.astype(jnp.float32), flat.astype(jnp.float32), (((0,), (1,)), ((), ())), preferred_element_type=jnp.float32)
    scores = scores - shift[:, None]
    return (mean, projector, scores.reshape(RANK, ROWS, COLS))
```

```python
import functools

import jax
import jax.numpy as jnp
from jax import lax
from jax.experimental import pallas as pl
from jax.experimental.pallas import tpu as pltpu
from jax.sharding import PartitionSpec as P

ITERS = 4
LANES = 128
HIGHEST = lax.Precision.HIGHEST

GAUSS = (0.0625, 0.25, 0.375, 0.25, 0.0625)


def padded_2(shard, sides, width):
    for axis, dim in sides:
        size, length = (lax.axis_size(axis), shard.shape[dim])
        up = [(i, (i + 1) % size) for i in range(size - 1)]
        down = [(j, i) for i, j in up]
        last = lax.slice_in_dim(shard, length - width, length, axis=dim)
        first = lax.slice_in_dim(shard, 0, width, axis=dim)
        before = lax.ppermute(last, axis, up)
        after = lax.ppermute(first, axis, down)
        shard = jnp.concatenate([before, shard, after], axis=dim)
    return shard


def edge_weight(first, count, total):
    position = first + jnp.arange(count, dtype=jnp.int32)
    weight = jnp.zeros((count,), jnp.float32)
    for offset in range(5):
        inside = (position + offset - 2 >= 0) & (position + offset - 2 < total)
        weight = weight + GAUSS[offset] * inside.astype(jnp.float32)
    return weight


def along_rows(padded, count):
    total = GAUSS[0] * padded[0:count].astype(jnp.float32)
    for offset in range(1, 5):
        total = total + GAUSS[offset] * padded[offset : offset + count].astype(jnp.float32)
    return total


def along_cols(padded, count):
    total = GAUSS[0] * padded[:, 0:count]
    for offset in range(1, 5):
        total = total + GAUSS[offset] * padded[:, offset : offset + count]
    return total


def pack_gram(gram, sums):
    n = gram.shape[0] // LANES
    row = lax.broadcasted_iota(jnp.int32, (LANES, LANES), 0)
    col = lax.broadcasted_iota(jnp.int32, (LANES, LANES), 1)
    blocks = []
    for i in range(n):
        for j in range(i, n):
            block = gram[i * LANES : (i + 1) * LANES, j * LANES : (j + 1) * LANES]
            if i == j:
                piece = sums[i * LANES : (i + 1) * LANES]
                block = jnp.where((row == LANES - 1) & (col < LANES - 1), piece[None, :], block)
                block = jnp.where((row == LANES - 2) & (col == 0), piece[LANES - 1], block)
            blocks.append(block)
    return jnp.concatenate(blocks, axis=0)


def all_sum(values):
    axes = ("row", "col")
    rows, cols = lax.axis_size("row"), lax.axis_size("col")
    if rows & (rows - 1) or cols & (cols - 1) or cols < 2:
        return lax.psum(values, axes)

    def pairs(row_bit, col_bit):
        return [(r * cols + c, (r ^ row_bit) * cols + (c ^ col_bit)) for r in range(rows) for c in range(cols)]

    core = pairs(0, 1)
    odd = lax.axis_index("col") % 2
    half = values.shape[0] // 2
    mine = lax.dynamic_slice_in_dim(values, odd * half, half)
    other = lax.dynamic_slice_in_dim(values, (1 - odd) * half, half)
    kept = mine + lax.ppermute(other, axes, core)
    row_steps = [pairs(1 << k, 0) for k in range(rows.bit_length() - 1)]
    col_steps = [pairs(0, 1 << k) for k in range(1, cols.bit_length() - 1)]
    order = row_steps[:1] + col_steps + row_steps[1:]
    swapped = list(order)
    for k in range(0, len(order) - 1, 2):
        swapped[k], swapped[k + 1] = order[k + 1], order[k]
    quarter = half // 2
    a, b = kept[:quarter], kept[quarter:]
    for first, second in zip(order, swapped):
        got_a = lax.ppermute(a, axes, first)
        got_b = lax.ppermute(b, axes, second)
        a = a + got_a
        b = b + got_b
    kept = jnp.concatenate([a, b])
    got = lax.ppermute(kept, axes, core)
    return jnp.where(odd == 0, jnp.concatenate([kept, got]), jnp.concatenate([got, kept]))


def inverse_factor(a):
    n = a.shape[0]
    row = lax.broadcasted_iota(jnp.int32, (n, n), 0)
    col = lax.broadcasted_iota(jnp.int32, (n, n), 1)
    work = jnp.concatenate([a, (row == col).astype(jnp.float32)], axis=1)
    blocks = [work[8 * i : 8 * i + 8] for i in range(n // 8)]
    sub = lax.broadcasted_iota(jnp.int32, (8, 2 * n), 0)
    ahead = 4
    pivots = []
    for j0 in range(0, n, ahead):
        first = j0 // 8
        cols = [[jnp.broadcast_to(b[:, j0 + k : j0 + k + 1], (8, 2 * n)) for b in blocks[first:]] for k in range(ahead)]
        for k in range(ahead):
            j = j0 + k
            s = j - 8 * first
            recip = 1.0 / jnp.broadcast_to(cols[k][0][s : s + 1], (8, 2 * n))
            pivots.append(recip)
            line = jnp.broadcast_to(blocks[first][s : s + 1], (8, 2 * n)) * recip
            factor = [c for c in cols[k]]
            factor[0] = jnp.where(sub > s, factor[0], 0.0)
            later = [jnp.broadcast_to(cols[m][0][s : s + 1], (8, 2 * n)) * recip for m in range(k + 1, ahead)]
            for i in range(first, n // 8):
                for m in range(k + 1, ahead):
                    cols[m][i - first] = cols[m][i - first] - factor[i - first] * later[m - k - 1]
                blocks[i] = blocks[i] - factor[i - first] * line
    out = []
    for i in range(n // 8):
        scale = jnp.zeros((8, 2 * n), jnp.float32)
        for s in range(8):
            scale = jnp.where(sub == s, pivots[8 * i + s], scale)
        out.append((blocks[i] * lax.rsqrt(1.0 / scale))[:, n:])
    return jnp.concatenate(out, axis=0)


def dot(a, b, contract, precision=HIGHEST):
    return lax.dot_general(a, b, (contract, ((), ())), precision=precision, preferred_element_type=jnp.float32)


def components_kernel(count, packed, start, smooth_hbm, mean_out, proj_out, scores_hbm, cov, smooth, scores, in_sem, out_sem):
    feat = cov.shape[0]
    n = feat // LANES
    rank = start.shape[1]
    tile_rows = smooth.shape[0]
    fetch = pltpu.make_async_copy(smooth_hbm, smooth, in_sem)
    fetch.start()
    row = lax.broadcasted_iota(jnp.int32, (LANES, LANES), 0)
    col = lax.broadcasted_iota(jnp.int32, (LANES, LANES), 1)
    lane = lax.broadcasted_iota(jnp.int32, (1, LANES), 1)
    inv = 1.0 / count
    index = {}
    for i in range(n):
        for j in range(i, n):
            index[i, j] = len(index)
    block = lambda i, j: packed[index[i, j] * LANES : (index[i, j] + 1) * LANES, :]
    means, mean_cols, diag = [], [], []
    for i in range(n):
        b = block(i, i)
        bt = b.T
        last = b[LANES - 2 : LANES - 1, 0:1]
        m = jnp.where(lane < LANES - 1, b[LANES - 1 : LANES, :], last) * inv
        means.append(m)
        mean_cols.append(jnp.broadcast_to(m, (LANES, LANES)).T)
        diag.append(jnp.where(row <= col, b, bt))
    mean = jnp.concatenate(means, axis=1)
    mean_out[...] = mean
    for i in range(n):
        for j in range(i, n):
            g = diag[i] if i == j else block(i, j)
            c = g * inv - mean_cols[i] * means[j]
            cov[i * LANES : (i + 1) * LANES, j * LANES : (j + 1) * LANES] = c
            if i != j:
                cov[j * LANES : (j + 1) * LANES, i * LANES : (i + 1) * LANES] = c.T
    basis = start[...].T
    for step in range(ITERS):
        y = dot(basis, cov[...], ((1,), (0,)))
        lower = inverse_factor(dot(y, y, ((1,), (1,))))
        basis = dot(lower, y, ((1,), (0,)))
    proj_out[...] = dot(basis, basis, ((0,), (0,)))
    basis_b = basis.astype(jnp.bfloat16)
    shift = jnp.sum(basis_b.astype(jnp.float32) * mean, axis=1, keepdims=True)
    shift = jnp.broadcast_to(shift, (rank, LANES))
    fetch.wait()
    for g in range(tile_rows // 8):
        for h in range(8 * g, 8 * g + 8):
            s = lax.dot_general(
                basis_b, smooth[h], (((1,), (1,)), ((), ())), preferred_element_type=jnp.float32
            )
            scores[:, h, :] = s - shift
        pltpu.make_async_copy(scores.at[:, pl.ds(8 * g, 8), :], scores_hbm.at[:, pl.ds(8 * g, 8), :], out_sem.at[g]).start()
    for g in range(tile_rows // 8):
        pltpu.make_async_copy(scores.at[:, pl.ds(8 * g, 8), :], scores_hbm.at[:, pl.ds(8 * g, 8), :], out_sem.at[g]).wait()


def components(packed, start, smoothed, count):
    tile_rows, tile_cols, feat = smoothed.shape
    rank = start.shape[1]
    vmem = pl.BlockSpec(memory_space=pltpu.VMEM)
    hbm = pl.BlockSpec(memory_space=pl.ANY)
    return pl.pallas_call(
        functools.partial(components_kernel, count),
        out_shape=(
            jax.ShapeDtypeStruct((1, feat), jnp.float32),
            jax.ShapeDtypeStruct((feat, feat), jnp.float32),
            jax.ShapeDtypeStruct((rank, tile_rows, tile_cols), jnp.float32),
        ),
        in_specs=[vmem, vmem, hbm],
        out_specs=(vmem, vmem, hbm),
        scratch_shapes=[
            pltpu.VMEM((feat, feat), jnp.float32),
            pltpu.VMEM((tile_rows, tile_cols, feat), jnp.bfloat16),
            pltpu.VMEM((rank, tile_rows, tile_cols), jnp.float32),
            pltpu.SemaphoreType.DMA,
            pltpu.SemaphoreType.DMA((tile_rows // 8,)),
        ],
        compiler_params=pltpu.CompilerParams(vmem_limit_bytes=32 << 20),
        cost_estimate=pl.CostEstimate(flops=10**9, bytes_accessed=10**7, transcendentals=0),
        name="components",
    )(packed, start, smoothed)


def local(pixels, start):
    tile_rows, tile_cols, feat = pixels.shape
    rows_total = tile_rows * lax.axis_size("row")
    cols_total = tile_cols * lax.axis_size("col")
    padded = padded_2(pixels, (("row", 0), ("col", 1)), 2)
    blurred = along_cols(along_rows(padded, tile_rows), tile_cols)
    row_weight = edge_weight(lax.axis_index("row") * tile_rows, tile_rows, rows_total)
    col_weight = edge_weight(lax.axis_index("col") * tile_cols, tile_cols, cols_total)
    weight = row_weight[:, None, None] * col_weight[None, :, None]
    smoothed = (blurred / weight).astype(jnp.bfloat16)
    flat = smoothed.reshape(tile_rows * tile_cols, feat)
    gram_local = lax.dot_general(
        flat, flat, (((0,), (0,)), ((), ())), preferred_element_type=jnp.float32
    )
    sums_local = jnp.sum(flat, axis=0, dtype=jnp.float32)
    packed = all_sum(pack_gram(gram_local, sums_local))
    mean, projector, scores = components(packed, start, smoothed, float(rows_total * cols_total))
    return (mean.reshape(feat), projector, scores)


def solution(mesh):
    in_specs = (P("row", "col", None), P())
    out_specs = (P(), P(), P(None, "row", "col"))
    return jax.shard_map(local, mesh=mesh, in_specs=in_specs, out_specs=out_specs, check_vma=False)
```

```python
import functools

import jax
import jax.numpy as jnp
from jax import lax
from jax.experimental import pallas as pl
from jax.experimental.pallas import tpu as pltpu
from jax.sharding import PartitionSpec as P

ITERS = 4
LANES = 128
HIGHEST = lax.Precision.HIGHEST

GAUSS = (0.0625, 0.25, 0.375, 0.25, 0.0625)


WIDTH = 2
HALO_ROWS = 16


def edges_2(shard, axis, dim):
    size, length = (lax.axis_size(axis), shard.shape[dim])
    up = [(i, i + 1) for i in range(size - 1)]
    down = [(j, i) for i, j in up]
    before = lax.ppermute(lax.slice_in_dim(shard, length - WIDTH, length, axis=dim), axis, up)
    after = lax.ppermute(lax.slice_in_dim(shard, 0, WIDTH, axis=dim), axis, down)
    return before, after


def edge_weight(first, count, total):
    position = first + jnp.arange(count, dtype=jnp.int32)
    weight = jnp.zeros((count,), jnp.float32)
    for offset in range(5):
        inside = (position + offset - 2 >= 0) & (position + offset - 2 < total)
        weight = weight + GAUSS[offset] * inside.astype(jnp.float32)
    return weight


def column_taps(count):
    out = jnp.arange(count, dtype=jnp.int32)[:, None]
    k = jnp.arange(count + HALO_ROWS, dtype=jnp.int32)[None, :]
    beside = k - count
    place = jnp.where(k < count, k, jnp.where(beside < WIDTH, beside - WIDTH, count + beside - WIDTH))
    place = jnp.where(beside < 2 * WIDTH, place, -count)
    taps = jnp.zeros((count, count + HALO_ROWS), jnp.float32)
    for offset in range(5):
        taps = jnp.where(place == out + offset - 2, GAUSS[offset], taps)
    return taps.astype(jnp.bfloat16)


def smooth_kernel(
    row_scale, pixels, above, below, left, right, taps, col_scale, smooth_hbm, packed,
    source, across, smooth, gram, sums, in_sem, out_sem,
):
    tile_rows, tile_cols, feat = pixels.shape
    group = 8
    groups = tile_rows // group
    span = tile_cols + HALO_ROWS

    def fetch(g):
        rows = pl.ds(g * group, group)
        there = source.at[pl.ds(g * group + WIDTH, group), pl.ds(0, tile_cols), :]
        return pltpu.make_async_copy(pixels.at[rows], there, in_sem.at[g])

    for g in range(groups):
        fetch(g).start()
    source[:, tile_cols:span, :] = jnp.zeros((tile_rows + 2 * WIDTH, HALO_ROWS, feat), jnp.bfloat16)
    source[0:WIDTH, 0:tile_cols, :] = above[...]
    source[tile_rows + WIDTH :, 0:tile_cols, :] = below[...]
    source[:, tile_cols : tile_cols + WIDTH, :] = left[...]
    source[:, tile_cols + WIDTH : tile_cols + 2 * WIDTH, :] = right[...]
    gram[...] = jnp.zeros_like(gram)
    sums[...] = jnp.zeros_like(sums)
    b = taps[...]

    def horizontal(r):
        across[r] = jnp.dot(b, source[r], preferred_element_type=jnp.float32)

    def vertical(g):
        sub = 16
        for i in range(tile_cols // sub):
            at = pl.ds(i * sub, sub)
            for f in range(feat // LANES):
                lanes = pl.ds(f * LANES, LANES)
                scale = col_scale[at, :]
                c = [across[g * group + r, at, lanes] for r in range(group + 4)]
                total = None
                for r in range(group):
                    v = c[r] + c[r + 4] + 4.0 * (c[r + 1] + c[r + 3]) + 6.0 * c[r + 2]
                    v = (v * (scale * row_scale[g * group + r])).astype(jnp.bfloat16)
                    smooth[g * group + r, at, lanes] = v
                    v = v.astype(jnp.float32)
                    total = v if total is None else total + v
                sums[:, lanes] += total

    def correlate(g):
        s = smooth[pl.ds(g * group, group)].reshape(group * tile_cols, feat)
        over = (((0,), (0,)), ((), ()))
        wide = feat - LANES
        gram[0:wide, 0:wide] += lax.dot_general(s[:, :wide], s[:, :wide], over, preferred_element_type=jnp.float32)
        gram[:, wide:] += lax.dot_general(s, s[:, wide:], over, preferred_element_type=jnp.float32)

    def send(g):
        rows = pl.ds(g * group, group)
        return pltpu.make_async_copy(smooth.at[rows], smooth_hbm.at[rows], out_sem.at[g])

    for r in range(WIDTH):
        horizontal(r)
        horizontal(tile_rows + WIDTH + r)
    fetch(0).wait()
    for r in range(group):
        horizontal(WIDTH + r)

    @pl.loop(0, groups)
    def _(g):
        @pl.when(g < groups - 1)
        def _():
            fetch(g + 1).wait()
            for r in range(group):
                horizontal((g + 1) * group + WIDTH + r)

        vertical(g)
        correlate(g)
        send(g).start()

    row = lax.broadcasted_iota(jnp.int32, (LANES, LANES), 0)
    col = lax.broadcasted_iota(jnp.int32, (LANES, LANES), 1)
    n = feat // LANES
    at = 0
    for i in range(n):
        for j in range(i, n):
            block = gram[i * LANES : (i + 1) * LANES, j * LANES : (j + 1) * LANES]
            if i == j:
                piece = jnp.sum(sums[:, i * LANES : (i + 1) * LANES], axis=0, keepdims=True)
                block = jnp.where((row == LANES - 1) & (col < LANES - 1), piece, block)
                block = jnp.where((row == LANES - 2) & (col == 0), piece[:, LANES - 1 : LANES], block)
            packed[at * LANES : (at + 1) * LANES, :] = block
            at += 1
    for g in range(groups):
        send(g).wait()


def smooth_and_gram(pixels, above, below, left, right, taps, row_scale, col_scale):
    tile_rows, tile_cols, feat = pixels.shape
    n = feat // LANES
    vmem = pl.BlockSpec(memory_space=pltpu.VMEM)
    hbm = pl.BlockSpec(memory_space=pl.ANY)
    smem = pl.BlockSpec(memory_space=pltpu.SMEM)
    return pl.pallas_call(
        smooth_kernel,
        out_shape=(
            jax.ShapeDtypeStruct(pixels.shape, jnp.bfloat16),
            jax.ShapeDtypeStruct((n * (n + 1) // 2 * LANES, LANES), jnp.float32),
        ),
        in_specs=[smem, hbm, vmem, vmem, vmem, vmem, vmem, vmem],
        out_specs=(hbm, vmem),
        scratch_shapes=[
            pltpu.VMEM((tile_rows + 4, tile_cols + HALO_ROWS, feat), jnp.bfloat16),
            pltpu.VMEM((tile_rows + 4, tile_cols, feat), jnp.float32),
            pltpu.VMEM(pixels.shape, jnp.bfloat16),
            pltpu.VMEM((feat, feat), jnp.float32),
            pltpu.VMEM((16, feat), jnp.float32),
            pltpu.SemaphoreType.DMA((tile_rows // 8,)),
            pltpu.SemaphoreType.DMA((tile_rows // 8,)),
        ],
        compiler_params=pltpu.CompilerParams(vmem_limit_bytes=40 << 20),
        cost_estimate=pl.CostEstimate(flops=5 * 10**9, bytes_accessed=2 * 10**7, transcendentals=0),
        name="smooth",
    )(row_scale, pixels, above, below, left, right, taps, col_scale)


def all_sum(values):
    axes = ("row", "col")
    rows, cols = lax.axis_size("row"), lax.axis_size("col")
    if rows & (rows - 1) or cols & (cols - 1) or cols < 2:
        return lax.psum(values, axes)

    def pairs(row_bit, col_bit):
        return [(r * cols + c, (r ^ row_bit) * cols + (c ^ col_bit)) for r in range(rows) for c in range(cols)]

    core = pairs(0, 1)
    odd = lax.axis_index("col") % 2
    half = values.shape[0] // 2
    mine = lax.dynamic_slice_in_dim(values, odd * half, half)
    other = lax.dynamic_slice_in_dim(values, (1 - odd) * half, half)
    kept = mine + lax.ppermute(other, axes, core)
    row_steps = [pairs(1 << k, 0) for k in range(rows.bit_length() - 1)]
    col_steps = [pairs(0, 1 << k) for k in range(1, cols.bit_length() - 1)]
    order = row_steps[:1] + col_steps + row_steps[1:]
    swapped = list(order)
    for k in range(0, len(order) - 1, 2):
        swapped[k], swapped[k + 1] = order[k + 1], order[k]
    quarter = half // 2
    a, b = kept[:quarter], kept[quarter:]
    for first, second in zip(order, swapped):
        got_a = lax.ppermute(a, axes, first)
        got_b = lax.ppermute(b, axes, second)
        a = a + got_a
        b = b + got_b
    kept = jnp.concatenate([a, b])
    got = lax.ppermute(kept, axes, core)
    return jnp.where(odd == 0, jnp.concatenate([kept, got]), jnp.concatenate([got, kept]))


def inverse_factor(a):
    n = a.shape[0]
    row = lax.broadcasted_iota(jnp.int32, (n, n), 0)
    col = lax.broadcasted_iota(jnp.int32, (n, n), 1)
    work = jnp.concatenate([a, (row == col).astype(jnp.float32)], axis=1)
    blocks = [work[8 * i : 8 * i + 8] for i in range(n // 8)]
    sub = lax.broadcasted_iota(jnp.int32, (8, 2 * n), 0)
    ahead = 4
    pivots = []
    for j0 in range(0, n, ahead):
        first = j0 // 8
        cols = [[jnp.broadcast_to(b[:, j0 + k : j0 + k + 1], (8, 2 * n)) for b in blocks[first:]] for k in range(ahead)]
        for k in range(ahead):
            j = j0 + k
            s = j - 8 * first
            recip = 1.0 / jnp.broadcast_to(cols[k][0][s : s + 1], (8, 2 * n))
            pivots.append(recip)
            line = jnp.broadcast_to(blocks[first][s : s + 1], (8, 2 * n)) * recip
            factor = [c for c in cols[k]]
            factor[0] = jnp.where(sub > s, factor[0], 0.0)
            later = [jnp.broadcast_to(cols[m][0][s : s + 1], (8, 2 * n)) * recip for m in range(k + 1, ahead)]
            for i in range(first, n // 8):
                for m in range(k + 1, ahead):
                    cols[m][i - first] = cols[m][i - first] - factor[i - first] * later[m - k - 1]
                blocks[i] = blocks[i] - factor[i - first] * line
    out = []
    for i in range(n // 8):
        scale = jnp.zeros((8, 2 * n), jnp.float32)
        for s in range(8):
            scale = jnp.where(sub == s, pivots[8 * i + s], scale)
        out.append((blocks[i] * lax.rsqrt(1.0 / scale))[:, n:])
    return jnp.concatenate(out, axis=0)


def dot(a, b, contract, precision=HIGHEST):
    return lax.dot_general(a, b, (contract, ((), ())), precision=precision, preferred_element_type=jnp.float32)


def components_kernel(count, packed, start, smooth_hbm, mean_out, proj_out, scores_hbm, cov, smooth, scores, in_sem, out_sem):
    feat = cov.shape[0]
    n = feat // LANES
    rank = start.shape[1]
    tile_rows = smooth.shape[0]
    fetch = pltpu.make_async_copy(smooth_hbm, smooth, in_sem)
    fetch.start()
    row = lax.broadcasted_iota(jnp.int32, (LANES, LANES), 0)
    col = lax.broadcasted_iota(jnp.int32, (LANES, LANES), 1)
    lane = lax.broadcasted_iota(jnp.int32, (1, LANES), 1)
    inv = 1.0 / count
    index = {}
    for i in range(n):
        for j in range(i, n):
            index[i, j] = len(index)
    block = lambda i, j: packed[index[i, j] * LANES : (index[i, j] + 1) * LANES, :]
    means, mean_cols, diag = [], [], []
    for i in range(n):
        b = block(i, i)
        bt = b.T
        last = b[LANES - 2 : LANES - 1, 0:1]
        m = jnp.where(lane < LANES - 1, b[LANES - 1 : LANES, :], last) * inv
        means.append(m)
        mean_cols.append(jnp.broadcast_to(m, (LANES, LANES)).T)
        diag.append(jnp.where(row <= col, b, bt))
    mean = jnp.concatenate(means, axis=1)
    mean_out[...] = mean
    for i in range(n):
        for j in range(i, n):
            g = diag[i] if i == j else block(i, j)
            c = g * inv - mean_cols[i] * means[j]
            cov[i * LANES : (i + 1) * LANES, j * LANES : (j + 1) * LANES] = c
            if i != j:
                cov[j * LANES : (j + 1) * LANES, i * LANES : (i + 1) * LANES] = c.T
    basis = start[...].T
    for step in range(ITERS):
        y = dot(basis, cov[...], ((1,), (0,)))
        lower = inverse_factor(dot(y, y, ((1,), (1,))))
        basis = dot(lower, y, ((1,), (0,)))
    proj_out[...] = dot(basis, basis, ((0,), (0,)))
    basis_b = basis.astype(jnp.bfloat16)
    shift = jnp.sum(basis_b.astype(jnp.float32) * mean, axis=1, keepdims=True)
    shift = jnp.broadcast_to(shift, (rank, LANES))
    fetch.wait()
    for g in range(tile_rows // 8):
        for h in range(8 * g, 8 * g + 8):
            s = lax.dot_general(
                basis_b, smooth[h], (((1,), (1,)), ((), ())), preferred_element_type=jnp.float32
            )
            scores[:, h, :] = s - shift
        pltpu.make_async_copy(scores.at[:, pl.ds(8 * g, 8), :], scores_hbm.at[:, pl.ds(8 * g, 8), :], out_sem.at[g]).start()
    for g in range(tile_rows // 8):
        pltpu.make_async_copy(scores.at[:, pl.ds(8 * g, 8), :], scores_hbm.at[:, pl.ds(8 * g, 8), :], out_sem.at[g]).wait()


def components(packed, start, smoothed, count):
    tile_rows, tile_cols, feat = smoothed.shape
    rank = start.shape[1]
    vmem = pl.BlockSpec(memory_space=pltpu.VMEM)
    hbm = pl.BlockSpec(memory_space=pl.ANY)
    return pl.pallas_call(
        functools.partial(components_kernel, count),
        out_shape=(
            jax.ShapeDtypeStruct((1, feat), jnp.float32),
            jax.ShapeDtypeStruct((feat, feat), jnp.float32),
            jax.ShapeDtypeStruct((rank, tile_rows, tile_cols), jnp.float32),
        ),
        in_specs=[vmem, vmem, hbm],
        out_specs=(vmem, vmem, hbm),
        scratch_shapes=[
            pltpu.VMEM((feat, feat), jnp.float32),
            pltpu.VMEM((tile_rows, tile_cols, feat), jnp.bfloat16),
            pltpu.VMEM((rank, tile_rows, tile_cols), jnp.float32),
            pltpu.SemaphoreType.DMA,
            pltpu.SemaphoreType.DMA((tile_rows // 8,)),
        ],
        compiler_params=pltpu.CompilerParams(vmem_limit_bytes=32 << 20),
        cost_estimate=pl.CostEstimate(flops=10**9, bytes_accessed=10**7, transcendentals=0),
        name="components",
    )(packed, start, smoothed)


def local(pixels, start):
    tile_rows, tile_cols, feat = pixels.shape
    rows_total = tile_rows * lax.axis_size("row")
    cols_total = tile_cols * lax.axis_size("col")
    above, below = edges_2(pixels, "row", 0)
    beside = [jnp.concatenate([above[:, c], pixels[:, c], below[:, c]], axis=0) for c in (slice(0, WIDTH), slice(tile_cols - WIDTH, tile_cols))]
    size = lax.axis_size("col")
    left = lax.ppermute(beside[1], "col", [(i, i + 1) for i in range(size - 1)])
    right = lax.ppermute(beside[0], "col", [(i + 1, i) for i in range(size - 1)])
    row_scale = GAUSS[0] / edge_weight(lax.axis_index("row") * tile_rows, tile_rows, rows_total)
    col_scale = 1.0 / edge_weight(lax.axis_index("col") * tile_cols, tile_cols, cols_total)
    col_scale = jnp.broadcast_to(col_scale[:, None], (tile_cols, LANES))
    smoothed, packed = smooth_and_gram(
        pixels, above, below, left, right, column_taps(tile_cols), row_scale, col_scale
    )
    packed = all_sum(packed)
    mean, projector, scores = components(packed, start, smoothed, float(rows_total * cols_total))
    return (mean.reshape(feat), projector, scores)


def solution(mesh):
    in_specs = (P("row", "col", None), P())
    out_specs = (P(), P(), P(None, "row", "col"))
    return jax.shard_map(local, mesh=mesh, in_specs=in_specs, out_specs=out_specs, check_vma=False)
```

```python
import functools

import jax
import jax.numpy as jnp
from jax import lax
from jax.experimental import pallas as pl
from jax.experimental.pallas import tpu as pltpu
from jax.sharding import PartitionSpec as P

ITERS = 4
LANES = 128
AHEAD = 16

GAUSS = (0.0625, 0.25, 0.375, 0.25, 0.0625)


WIDTH = 2
HALO_ROWS = 16


def edges_2(shard, axis, dim):
    size, length = (lax.axis_size(axis), shard.shape[dim])
    up = [(i, i + 1) for i in range(size - 1)]
    down = [(j, i) for i, j in up]
    before = lax.ppermute(lax.slice_in_dim(shard, length - WIDTH, length, axis=dim), axis, up)
    after = lax.ppermute(lax.slice_in_dim(shard, 0, WIDTH, axis=dim), axis, down)
    return before, after


def edge_weight(first, count, total):
    position = first + jnp.arange(count, dtype=jnp.int32)
    weight = jnp.zeros((count,), jnp.float32)
    for offset in range(5):
        inside = (position + offset - 2 >= 0) & (position + offset - 2 < total)
        weight = weight + GAUSS[offset] * inside.astype(jnp.float32)
    return weight


def column_taps(count):
    out = jnp.arange(count, dtype=jnp.int32)[:, None]
    k = jnp.arange(count + HALO_ROWS, dtype=jnp.int32)[None, :]
    beside = k - count
    place = jnp.where(k < count, k, jnp.where(beside < WIDTH, beside - WIDTH, count + beside - WIDTH))
    place = jnp.where(beside < 2 * WIDTH, place, -count)
    taps = jnp.zeros((count, count + HALO_ROWS), jnp.float32)
    for offset in range(5):
        taps = jnp.where(place == out + offset - 2, GAUSS[offset], taps)
    return taps.astype(jnp.bfloat16)


def smooth_kernel(
    row_scale, pixels, above, below, left, right, taps, col_scale, smooth_hbm, packed,
    source, across, smooth, gram, sums, in_sem, out_sem,
):
    tile_rows, tile_cols, feat = pixels.shape
    group = 8
    groups = tile_rows // group
    span = tile_cols + HALO_ROWS

    def fetch(g):
        rows = pl.ds(g * group, group)
        there = source.at[pl.ds(g * group + WIDTH, group), pl.ds(0, tile_cols), :]
        return pltpu.make_async_copy(pixels.at[rows], there, in_sem.at[g])

    for g in range(groups):
        fetch(g).start()
    source[:, tile_cols:span, :] = jnp.zeros((tile_rows + 2 * WIDTH, HALO_ROWS, feat), jnp.bfloat16)
    source[0:WIDTH, 0:tile_cols, :] = above[...]
    source[tile_rows + WIDTH :, 0:tile_cols, :] = below[...]
    source[:, tile_cols : tile_cols + WIDTH, :] = left[...]
    source[:, tile_cols + WIDTH : tile_cols + 2 * WIDTH, :] = right[...]
    gram[...] = jnp.zeros_like(gram)
    sums[...] = jnp.zeros_like(sums)
    b = taps[...]

    def horizontal(r):
        across[r] = jnp.dot(b, source[r], preferred_element_type=jnp.float32)

    def vertical(g):
        sub = 16
        for i in range(tile_cols // sub):
            at = pl.ds(i * sub, sub)
            for f in range(feat // LANES):
                lanes = pl.ds(f * LANES, LANES)
                scale = col_scale[at, :]
                c = [across[g * group + r, at, lanes] for r in range(group + 4)]
                total = None
                for r in range(group):
                    v = c[r] + c[r + 4] + 4.0 * (c[r + 1] + c[r + 3]) + 6.0 * c[r + 2]
                    v = (v * (scale * row_scale[g * group + r])).astype(jnp.bfloat16)
                    smooth[g * group + r, at, lanes] = v
                    v = v.astype(jnp.float32)
                    total = v if total is None else total + v
                sums[:, lanes] += total

    def correlate(g):
        s = smooth[pl.ds(g * group, group)].reshape(group * tile_cols, feat)
        over = (((0,), (0,)), ((), ()))
        wide = feat - LANES
        gram[0:wide, 0:wide] += lax.dot_general(s[:, :wide], s[:, :wide], over, preferred_element_type=jnp.float32)
        gram[:, wide:] += lax.dot_general(s, s[:, wide:], over, preferred_element_type=jnp.float32)

    def send(g):
        rows = pl.ds(g * group, group)
        return pltpu.make_async_copy(smooth.at[rows], smooth_hbm.at[rows], out_sem.at[g])

    for r in range(WIDTH):
        horizontal(r)
        horizontal(tile_rows + WIDTH + r)
    fetch(0).wait()
    for r in range(group):
        horizontal(WIDTH + r)

    @pl.loop(0, groups)
    def _(g):
        @pl.when(g < groups - 1)
        def _():
            fetch(g + 1).wait()
            for r in range(group):
                horizontal((g + 1) * group + WIDTH + r)

        vertical(g)
        correlate(g)
        send(g).start()

    row = lax.broadcasted_iota(jnp.int32, (LANES, LANES), 0)
    col = lax.broadcasted_iota(jnp.int32, (LANES, LANES), 1)
    n = feat // LANES
    at = 0
    for i in range(n):
        for j in range(i, n):
            block = gram[i * LANES : (i + 1) * LANES, j * LANES : (j + 1) * LANES]
            if i == j:
                piece = jnp.sum(sums[:, i * LANES : (i + 1) * LANES], axis=0, keepdims=True)
                block = jnp.where((row == LANES - 1) & (col < LANES - 1), piece, block)
                block = jnp.where((row == LANES - 2) & (col == 0), piece[:, LANES - 1 : LANES], block)
            packed[at * LANES : (at + 1) * LANES, :] = block
            at += 1
    for g in range(groups):
        send(g).wait()


def smooth_and_gram(pixels, above, below, left, right, taps, row_scale, col_scale):
    tile_rows, tile_cols, feat = pixels.shape
    n = feat // LANES
    vmem = pl.BlockSpec(memory_space=pltpu.VMEM)
    hbm = pl.BlockSpec(memory_space=pltpu.HBM)
    smem = pl.BlockSpec(memory_space=pltpu.SMEM)
    return pl.pallas_call(
        smooth_kernel,
        out_shape=(
            jax.ShapeDtypeStruct(pixels.shape, jnp.bfloat16),
            jax.ShapeDtypeStruct((n * (n + 1) // 2 * LANES, LANES), jnp.float32),
        ),
        in_specs=[smem, hbm, vmem, vmem, vmem, vmem, vmem, vmem],
        out_specs=(hbm, vmem),
        scratch_shapes=[
            pltpu.VMEM((tile_rows + 4, tile_cols + HALO_ROWS, feat), jnp.bfloat16),
            pltpu.VMEM((tile_rows + 4, tile_cols, feat), jnp.float32),
            pltpu.VMEM(pixels.shape, jnp.bfloat16),
            pltpu.VMEM((feat, feat), jnp.float32),
            pltpu.VMEM((16, feat), jnp.float32),
            pltpu.SemaphoreType.DMA((tile_rows // 8,)),
            pltpu.SemaphoreType.DMA((tile_rows // 8,)),
        ],
        compiler_params=pltpu.CompilerParams(vmem_limit_bytes=40 << 20),
        cost_estimate=pl.CostEstimate(flops=5 * 10**9, bytes_accessed=2 * 10**7, transcendentals=0),
        name="smooth",
    )(row_scale, pixels, above, below, left, right, taps, col_scale)


def all_sum(values):
    axes = ("row", "col")
    rows, cols = lax.axis_size("row"), lax.axis_size("col")
    if rows & (rows - 1) or cols & (cols - 1) or cols < 2:
        return lax.psum(values, axes)

    def pairs(row_bit, col_bit):
        return [(r * cols + c, (r ^ row_bit) * cols + (c ^ col_bit)) for r in range(rows) for c in range(cols)]

    core = pairs(0, 1)
    odd = lax.axis_index("col") % 2
    half = values.shape[0] // 2
    mine = lax.dynamic_slice_in_dim(values, odd * half, half)
    other = lax.dynamic_slice_in_dim(values, (1 - odd) * half, half)
    kept = mine + lax.ppermute(other, axes, core)
    row_steps = [pairs(1 << k, 0) for k in range(rows.bit_length() - 1)]
    col_steps = [pairs(0, 1 << k) for k in range(1, cols.bit_length() - 1)]
    order = row_steps[:1] + col_steps + row_steps[1:]
    swapped = list(order)
    for k in range(0, len(order) - 1, 2):
        swapped[k], swapped[k + 1] = order[k + 1], order[k]
    quarter = half // 2
    a, b = kept[:quarter], kept[quarter:]
    for first, second in zip(order, swapped):
        got_a = lax.ppermute(a, axes, first)
        got_b = lax.ppermute(b, axes, second)
        a = a + got_a
        b = b + got_b
    kept = jnp.concatenate([a, b])
    got = lax.ppermute(kept, axes, core)
    return jnp.where(odd == 0, jnp.concatenate([kept, got]), jnp.concatenate([got, kept]))


def inverse_factor(a):
    n = a.shape[0]
    row = lax.broadcasted_iota(jnp.int32, (n, n), 0)
    col = lax.broadcasted_iota(jnp.int32, (n, n), 1)
    work = jnp.concatenate([a, (row == col).astype(jnp.float32)], axis=1)
    blocks = [work[8 * i : 8 * i + 8] for i in range(n // 8)]
    sub = lax.broadcasted_iota(jnp.int32, (8, 2 * n), 0)
    ahead = min(AHEAD, n)
    pivots = []
    for j0 in range(0, n, ahead):
        first = j0 // 8
        cols = [
            {i: jnp.broadcast_to(blocks[i][:, j : j + 1], (8, 2 * n)) for i in range(j // 8, n // 8)}
            for j in range(j0, j0 + ahead)
        ]
        for k in range(ahead):
            j = j0 + k
            top = j // 8
            s = j - 8 * top
            recip = 1.0 / jnp.broadcast_to(cols[k][top][s : s + 1], (8, 2 * n))
            pivots.append(recip)
            factor = dict(cols[k])
            factor[top] = jnp.where(sub > s, factor[top], 0.0)
            for m in range(k + 1, ahead):
                other = (j0 + m) // 8
                t = j0 + m - 8 * other
                scaled = jnp.broadcast_to(cols[k][other][t : t + 1], (8, 2 * n)) * recip
                for i in cols[m]:
                    cols[m][i] = cols[m][i] - factor[i] * scaled
            line = jnp.broadcast_to(blocks[top][s : s + 1], (8, 2 * n)) * recip
            for i in range(top, n // 8):
                blocks[i] = blocks[i] - factor[i] * line
    out = []
    for i in range(n // 8):
        scale = pivots[8 * i]
        for s in range(1, 8):
            scale = jnp.where(sub == s, pivots[8 * i + s], scale)
        out.append((blocks[i] * lax.sqrt(scale))[:, n:])
    return jnp.concatenate(out, axis=0)


def thirds(x):
    high = x.astype(jnp.bfloat16)
    rest = x - high.astype(jnp.float32)
    middle = rest.astype(jnp.bfloat16)
    return high, middle, (rest - middle.astype(jnp.float32)).astype(jnp.bfloat16)


def dot(a, b, contract):
    return lax.dot_general(a, b, (contract, ((), ())), preferred_element_type=jnp.float32)


def dot_thirds(a, b):
    m = a[0].shape[0]
    one = dot(jnp.concatenate(a, axis=0), b[0], ((1,), (0,)))
    two = dot(jnp.concatenate(a[:2], axis=0), b[1], ((1,), (0,)))
    low = one[2 * m :] + two[m:] + dot(a[0], b[2], ((1,), (0,)))
    return one[:m] + (one[m : 2 * m] + two[:m] + low)


def gram_thirds(y):
    m = y[0].shape[0]
    stack = jnp.concatenate(y, axis=0)
    p = dot(stack, stack, ((1,), (1,)))
    part = lambda i, j: p[i * m : (i + 1) * m, j * m : (j + 1) * m]
    return part(0, 0) + ((part(0, 1) + part(1, 0)) + (part(1, 1) + (part(0, 2) + part(2, 0))))


def components_kernel(count, packed, start, smooth_hbm, mean_out, proj_out, scores_hbm, cov, smooth, scores, in_sem, out_sem):
    feat = cov.shape[0]
    n = feat // LANES
    rank = start.shape[1]
    tile_rows = smooth.shape[0]
    fetch = pltpu.make_async_copy(smooth_hbm, smooth, in_sem)
    fetch.start()
    row = lax.broadcasted_iota(jnp.int32, (LANES, LANES), 0)
    col = lax.broadcasted_iota(jnp.int32, (LANES, LANES), 1)
    lane = lax.broadcasted_iota(jnp.int32, (1, LANES), 1)
    inv = 1.0 / count
    index = {}
    for i in range(n):
        for j in range(i, n):
            index[i, j] = len(index)
    block = lambda i, j: packed[index[i, j] * LANES : (index[i, j] + 1) * LANES, :]
    means, mean_cols, diag = [], [], []
    for i in range(n):
        b = block(i, i)
        bt = b.T
        last = b[LANES - 2 : LANES - 1, 0:1]
        m = jnp.where(lane < LANES - 1, b[LANES - 1 : LANES, :], last) * inv
        means.append(m)
        mean_cols.append(jnp.broadcast_to(m, (LANES, LANES)).T)
        diag.append(jnp.where(row <= col, b, bt))
    mean = jnp.concatenate(means, axis=1)
    mean_out[...] = mean
    for i in range(n):
        for j in range(i, n):
            g = diag[i] if i == j else block(i, j)
            c = g * inv - mean_cols[i] * means[j]
            cov[i * LANES : (i + 1) * LANES, j * LANES : (j + 1) * LANES] = c
            if i != j:
                cov[j * LANES : (j + 1) * LANES, i * LANES : (i + 1) * LANES] = c.T
    cov_thirds = thirds(cov[...])
    y = dot_thirds(thirds(start[...].T), cov_thirds)
    for step in range(ITERS):
        parts = thirds(y)
        z = y if step == ITERS - 1 else dot_thirds(parts, cov_thirds)
        lower = inverse_factor(gram_thirds(parts))
        y = dot_thirds(thirds(lower), thirds(z))
    basis = y
    b = thirds(basis)
    left = jnp.concatenate([b[0], b[0], b[1], b[1], b[0], b[2]], axis=0)
    right = jnp.concatenate([b[0], b[1], b[0], b[1], b[2], b[0]], axis=0)
    proj_out[...] = dot(left, right, ((0,), (0,)))
    basis_b = basis.astype(jnp.bfloat16)
    shift = jnp.sum(basis_b.astype(jnp.float32) * mean, axis=1, keepdims=True)
    shift = jnp.broadcast_to(shift, (rank, LANES))
    fetch.wait()
    for g in range(tile_rows // 8):
        for h in range(8 * g, 8 * g + 8):
            s = lax.dot_general(
                basis_b, smooth[h], (((1,), (1,)), ((), ())), preferred_element_type=jnp.float32
            )
            scores[:, h, :] = s - shift
        pltpu.make_async_copy(scores.at[:, pl.ds(8 * g, 8), :], scores_hbm.at[:, pl.ds(8 * g, 8), :], out_sem.at[g]).start()
    for g in range(tile_rows // 8):
        pltpu.make_async_copy(scores.at[:, pl.ds(8 * g, 8), :], scores_hbm.at[:, pl.ds(8 * g, 8), :], out_sem.at[g]).wait()


def components(packed, start, smoothed, count):
    tile_rows, tile_cols, feat = smoothed.shape
    rank = start.shape[1]
    vmem = pl.BlockSpec(memory_space=pltpu.VMEM)
    hbm = pl.BlockSpec(memory_space=pltpu.HBM)
    return pl.pallas_call(
        functools.partial(components_kernel, count),
        out_shape=(
            jax.ShapeDtypeStruct((1, feat), jnp.float32),
            jax.ShapeDtypeStruct((feat, feat), jnp.float32),
            jax.ShapeDtypeStruct((rank, tile_rows, tile_cols), jnp.float32),
        ),
        in_specs=[vmem, vmem, hbm],
        out_specs=(vmem, vmem, hbm),
        scratch_shapes=[
            pltpu.VMEM((feat, feat), jnp.float32),
            pltpu.VMEM((tile_rows, tile_cols, feat), jnp.bfloat16),
            pltpu.VMEM((rank, tile_rows, tile_cols), jnp.float32),
            pltpu.SemaphoreType.DMA,
            pltpu.SemaphoreType.DMA((tile_rows // 8,)),
        ],
        compiler_params=pltpu.CompilerParams(vmem_limit_bytes=32 << 20),
        cost_estimate=pl.CostEstimate(flops=10**9, bytes_accessed=10**7, transcendentals=0),
        name="components",
    )(packed, start, smoothed)


def local(pixels, start):
    tile_rows, tile_cols, feat = pixels.shape
    rows_total = tile_rows * lax.axis_size("row")
    cols_total = tile_cols * lax.axis_size("col")
    above, below = edges_2(pixels, "row", 0)
    beside = [jnp.concatenate([above[:, c], pixels[:, c], below[:, c]], axis=0) for c in (slice(0, WIDTH), slice(tile_cols - WIDTH, tile_cols))]
    size = lax.axis_size("col")
    left = lax.ppermute(beside[1], "col", [(i, i + 1) for i in range(size - 1)])
    right = lax.ppermute(beside[0], "col", [(i + 1, i) for i in range(size - 1)])
    row_scale = GAUSS[0] / edge_weight(lax.axis_index("row") * tile_rows, tile_rows, rows_total)
    col_scale = 1.0 / edge_weight(lax.axis_index("col") * tile_cols, tile_cols, cols_total)
    col_scale = jnp.broadcast_to(col_scale[:, None], (tile_cols, LANES))
    smoothed, packed = smooth_and_gram(
        pixels, above, below, left, right, column_taps(tile_cols), row_scale, col_scale
    )
    packed = all_sum(packed)
    mean, projector, scores = components(packed, start, smoothed, float(rows_total * cols_total))
    return (mean.reshape(feat), projector, scores)


def solution(mesh):
    in_specs = (P("row", "col", None), P())
    out_specs = (P(), P(), P(None, "row", "col"))
    return jax.shard_map(local, mesh=mesh, in_specs=in_specs, out_specs=out_specs, check_vma=False)
```

```python
import functools

import jax
import jax.numpy as jnp
from jax import lax
from jax.experimental import pallas as pl
from jax.experimental.pallas import tpu as pltpu
from jax.sharding import PartitionSpec as P

ITERS = 4
LANES = 128
AHEAD = 16
CHUNK = 4
FLAGS = {}

GAUSS = (0.0625, 0.25, 0.375, 0.25, 0.0625)


WIDTH = 2
HALO_ROWS = 16


def edges_2(shard, axis, dim):
    size, length = (lax.axis_size(axis), shard.shape[dim])
    up = [(i, i + 1) for i in range(size - 1)]
    down = [(j, i) for i, j in up]
    before = lax.ppermute(lax.slice_in_dim(shard, length - WIDTH, length, axis=dim), axis, up)
    after = lax.ppermute(lax.slice_in_dim(shard, 0, WIDTH, axis=dim), axis, down)
    return before, after


def edge_weight(first, count, total):
    position = first + jnp.arange(count, dtype=jnp.int32)
    weight = jnp.zeros((count,), jnp.float32)
    for offset in range(5):
        inside = (position + offset - 2 >= 0) & (position + offset - 2 < total)
        weight = weight + GAUSS[offset] * inside.astype(jnp.float32)
    return weight


def column_taps(count):
    out = jnp.arange(count, dtype=jnp.int32)[:, None]
    k = jnp.arange(count + HALO_ROWS, dtype=jnp.int32)[None, :]
    beside = k - count
    place = jnp.where(k < count, k, jnp.where(beside < WIDTH, beside - WIDTH, count + beside - WIDTH))
    place = jnp.where(beside < 2 * WIDTH, place, -count)
    taps = jnp.zeros((count, count + HALO_ROWS), jnp.float32)
    for offset in range(5):
        taps = jnp.where(place == out + offset - 2, GAUSS[offset], taps)
    return taps.astype(jnp.bfloat16)


def smooth_kernel(
    row_scale, pixels, above, below, left, right, taps, col_scale, smooth_hbm, packed,
    source, across, rounded, smooth, gram, ends, in_sem, out_sem,
):
    tile_rows, tile_cols, feat = pixels.shape
    group = 8
    groups = tile_rows // group
    span = tile_cols + HALO_ROWS
    strip = tile_cols // group

    def fetch(g):
        there = source.at[pl.ds(g * group + WIDTH, group), pl.ds(0, tile_cols), :]
        return pltpu.make_async_copy(pixels.at[pl.ds(g * group, group)], there, in_sem.at[g])

    def send(g):
        rows = pl.ds(g * group, group)
        return pltpu.make_async_copy(smooth.at[rows], smooth_hbm.at[rows], out_sem.at[g])

    for g in range(groups):
        fetch(g).start()
    source[:, tile_cols:span, :] = jnp.zeros((tile_rows + 2 * WIDTH, HALO_ROWS, feat), jnp.bfloat16)
    source[0:WIDTH, 0:tile_cols, :] = above[...]
    source[tile_rows + WIDTH :, 0:tile_cols, :] = below[...]
    source[:, tile_cols : tile_cols + WIDTH, :] = left[...]
    source[:, tile_cols + WIDTH : tile_cols + 2 * WIDTH, :] = right[...]
    gram[...] = jnp.zeros_like(gram)
    ends[...] = jnp.zeros_like(ends)

    def horizontal(g, q):
        across[g % 4, q] = jnp.dot(taps[...], source[group * g + 4 + q], preferred_element_type=jnp.float32)

    def vertical(g, i):
        at = slice(i * strip, (i + 1) * strip)
        scales = [col_scale[at, :] * row_scale[g * group + r] for r in range(group)]
        for f in range(feat // LANES):
            lanes = slice(f * LANES, (f + 1) * LANES)
            c = [across[(g - 1) % 4, 4 + r, at, lanes] for r in range(4)]
            c += [across[g % 4, r, at, lanes] for r in range(group)]
            for _ in range(4):
                c = [p + q for p, q in zip(c, c[1:])]
            for r in range(group):
                v = (c[r] * scales[r]).astype(jnp.bfloat16)
                smooth[g * group + r, at, lanes] = v
                rounded[g % 2, r, at, lanes] = v

    def correlate(g, first, count):
        s = rounded[g % 2, first : first + count].reshape(count * tile_cols, feat)
        over = (((0,), (0,)), ((), ()))
        wide = feat - LANES
        last = jnp.concatenate([s[:, wide:], jnp.ones((count * tile_cols, LANES), jnp.bfloat16)], axis=1)
        gram[...] += lax.dot_general(s[:, :wide], s[:, :wide], over, preferred_element_type=jnp.float32)
        ends[...] += lax.dot_general(s, last, over, preferred_element_type=jnp.float32)

    fetch(0).wait()
    for q in range(4, group):
        horizontal(-1, q)
    fetch(1).wait()
    for q in range(group):
        horizontal(0, q)
    for g in range(groups + 1):
        if g + 2 < groups:
            fetch(g + 2).wait()
        for q in range(group):
            if g + 1 < groups:
                horizontal(g + 1, q)
            if g < groups:
                vertical(g, q)
            if g > 0 and q % CHUNK == CHUNK - 1:
                correlate(g - 1, q - CHUNK + 1, CHUNK)
        if g < groups:
            send(g).start()

    row = lax.broadcasted_iota(jnp.int32, (LANES, LANES), 0)
    col = lax.broadcasted_iota(jnp.int32, (LANES, LANES), 1)
    n = feat // LANES
    at = 0
    for i in range(n):
        for j in range(i, n):
            rows = slice(i * LANES, (i + 1) * LANES)
            block = ends[rows, :LANES] if j == n - 1 else gram[rows, j * LANES : (j + 1) * LANES]
            if i == j:
                piece = ends[rows, LANES:]
                block = jnp.where((col == 0) & (row > 0), piece, block)
                block = jnp.where((col == 1) & (row == LANES - 1), piece[0:1, :], block)
            packed[at * LANES : (at + 1) * LANES, :] = block
            at += 1
    for g in range(groups):
        send(g).wait()


def smooth_and_gram(pixels, above, below, left, right, taps, row_scale, col_scale):
    tile_rows, tile_cols, feat = pixels.shape
    n = feat // LANES
    vmem = pl.BlockSpec(memory_space=pltpu.VMEM)
    hbm = pl.BlockSpec(memory_space=pltpu.HBM)
    smem = pl.BlockSpec(memory_space=pltpu.SMEM)
    return pl.pallas_call(
        smooth_kernel,
        out_shape=(
            pltpu.HBM(pixels.shape, jnp.bfloat16),
            jax.ShapeDtypeStruct((n * (n + 1) // 2 * LANES, LANES), jnp.float32),
        ),
        in_specs=[smem, hbm, vmem, vmem, vmem, vmem, vmem, vmem],
        out_specs=(hbm, vmem),
        scratch_shapes=[
            pltpu.VMEM((tile_rows + 4, tile_cols + HALO_ROWS, feat), jnp.bfloat16),
            pltpu.VMEM((4, 8, tile_cols, feat), jnp.float32),
            pltpu.VMEM((2, 8, tile_cols, feat), jnp.bfloat16),
            pltpu.VMEM(pixels.shape, jnp.bfloat16),
            pltpu.VMEM((feat - LANES, feat - LANES), jnp.float32),
            pltpu.VMEM((feat, 2 * LANES), jnp.float32),
            pltpu.SemaphoreType.DMA((tile_rows // 8,)),
            pltpu.SemaphoreType.DMA((tile_rows // 8,)),
        ],
        compiler_params=pltpu.CompilerParams(vmem_limit_bytes=40 << 20, flags=FLAGS),
        cost_estimate=pl.CostEstimate(flops=5 * 10**9, bytes_accessed=2 * 10**7, transcendentals=0),
        name="smooth",
    )(row_scale, pltpu.with_memory_space_constraint(pixels, pltpu.HBM), above, below, left, right, taps, col_scale)


def all_sum(values):
    axes = ("row", "col")
    rows, cols = lax.axis_size("row"), lax.axis_size("col")
    if rows & (rows - 1) or cols & (cols - 1) or cols < 2:
        return lax.psum(values, axes)

    def pairs(row_bit, col_bit):
        return [(r * cols + c, (r ^ row_bit) * cols + (c ^ col_bit)) for r in range(rows) for c in range(cols)]

    core = pairs(0, 1)
    odd = lax.axis_index("col") % 2
    half = values.shape[0] // 2
    mine = lax.dynamic_slice_in_dim(values, odd * half, half)
    other = lax.dynamic_slice_in_dim(values, (1 - odd) * half, half)
    kept = mine + lax.ppermute(other, axes, core)
    row_steps = [pairs(1 << k, 0) for k in range(rows.bit_length() - 1)]
    col_steps = [pairs(0, 1 << k) for k in range(1, cols.bit_length() - 1)]
    order = row_steps[:1] + col_steps + row_steps[1:]
    swapped = list(order)
    for k in range(0, len(order) - 1, 2):
        swapped[k], swapped[k + 1] = order[k + 1], order[k]
    quarter = half // 2
    a, b = kept[:quarter], kept[quarter:]
    for first, second in zip(order, swapped):
        got_a = lax.ppermute(a, axes, first)
        got_b = lax.ppermute(b, axes, second)
        a = a + got_a
        b = b + got_b
    kept = jnp.concatenate([a, b])
    got = lax.ppermute(kept, axes, core)
    return jnp.where(odd == 0, jnp.concatenate([kept, got]), jnp.concatenate([got, kept]))


def inverse_factor(a):
    n = a.shape[0]
    row = lax.broadcasted_iota(jnp.int32, (n, n), 0)
    col = lax.broadcasted_iota(jnp.int32, (n, n), 1)
    work = jnp.concatenate([a, (row == col).astype(jnp.float32)], axis=1)
    blocks = [work[8 * i : 8 * i + 8] for i in range(n // 8)]
    sub = lax.broadcasted_iota(jnp.int32, (8, 2 * n), 0)
    ahead = min(AHEAD, n)
    pivots = []
    for j0 in range(0, n, ahead):
        first = j0 // 8
        cols = [
            {i: jnp.broadcast_to(blocks[i][:, j : j + 1], (8, 2 * n)) for i in range(j // 8, n // 8)}
            for j in range(j0, j0 + ahead)
        ]
        for k in range(ahead):
            j = j0 + k
            top = j // 8
            s = j - 8 * top
            recip = 1.0 / jnp.broadcast_to(cols[k][top][s : s + 1], (8, 2 * n))
            pivots.append(recip)
            factor = dict(cols[k])
            factor[top] = jnp.where(sub > s, factor[top], 0.0)
            for m in range(k + 1, ahead):
                other = (j0 + m) // 8
                t = j0 + m - 8 * other
                scaled = jnp.broadcast_to(cols[k][other][t : t + 1], (8, 2 * n)) * recip
                for i in cols[m]:
                    cols[m][i] = cols[m][i] - factor[i] * scaled
            line = jnp.broadcast_to(blocks[top][s : s + 1], (8, 2 * n)) * recip
            for i in range(top, n // 8):
                blocks[i] = blocks[i] - factor[i] * line
    out = []
    for i in range(n // 8):
        scale = pivots[8 * i]
        for s in range(1, 8):
            scale = jnp.where(sub == s, pivots[8 * i + s], scale)
        out.append((blocks[i] * lax.sqrt(scale))[:, n:])
    return jnp.concatenate(out, axis=0)


def thirds(x):
    high = x.astype(jnp.bfloat16)
    rest = x - high.astype(jnp.float32)
    middle = rest.astype(jnp.bfloat16)
    return high, middle, (rest - middle.astype(jnp.float32)).astype(jnp.bfloat16)


def dot(a, b, contract):
    return lax.dot_general(a, b, (contract, ((), ())), preferred_element_type=jnp.float32)


def dot_thirds(a, b):
    m = a[0].shape[0]
    one = dot(jnp.concatenate(a, axis=0), b[0], ((1,), (0,)))
    two = dot(jnp.concatenate(a[:2], axis=0), b[1], ((1,), (0,)))
    low = one[2 * m :] + two[m:] + dot(a[0], b[2], ((1,), (0,)))
    return one[:m] + (one[m : 2 * m] + two[:m] + low)


def gram_thirds(y):
    m = y[0].shape[0]
    stack = jnp.concatenate(y, axis=0)
    p = dot(stack, stack, ((1,), (1,)))
    part = lambda i, j: p[i * m : (i + 1) * m, j * m : (j + 1) * m]
    return part(0, 0) + ((part(0, 1) + part(1, 0)) + (part(1, 1) + (part(0, 2) + part(2, 0))))


def components_kernel(count, packed, start, smooth_hbm, mean_out, proj_out, scores_hbm, cov, smooth, scores, in_sem, out_sem):
    feat = cov.shape[0]
    n = feat // LANES
    rank = start.shape[1]
    tile_rows = smooth.shape[0]
    fetch = pltpu.make_async_copy(smooth_hbm, smooth, in_sem)
    fetch.start()
    row = lax.broadcasted_iota(jnp.int32, (LANES, LANES), 0)
    col = lax.broadcasted_iota(jnp.int32, (LANES, LANES), 1)
    inv = 1.0 / count
    index = {}
    for i in range(n):
        for j in range(i, n):
            index[i, j] = len(index)
    block = lambda i, j: packed[index[i, j] * LANES : (index[i, j] + 1) * LANES, :]
    means, mean_cols, diag = [], [], []
    for i in range(n):
        b = block(i, i)
        bt = b.T
        first = jnp.broadcast_to(b[LANES - 1 : LANES, 1:2], (LANES, LANES))
        m = jnp.where(row > 0, jnp.broadcast_to(b[:, 0:1], (LANES, LANES)), first) * inv
        means.append(m.T[0:1, :])
        mean_cols.append(m)
        diag.append(jnp.where(row <= col, b, bt))
    mean = jnp.concatenate(means, axis=1)
    mean_out[...] = mean
    for i in range(n):
        for j in range(i, n):
            g = diag[i] if i == j else block(i, j)
            c = g * inv - mean_cols[i] * means[j]
            cov[i * LANES : (i + 1) * LANES, j * LANES : (j + 1) * LANES] = c
            if i != j:
                cov[j * LANES : (j + 1) * LANES, i * LANES : (i + 1) * LANES] = c.T
    cov_thirds = thirds(cov[...])
    y = dot_thirds(thirds(start[...].T), cov_thirds)
    for step in range(ITERS):
        parts = thirds(y)
        z = y if step == ITERS - 1 else dot_thirds(parts, cov_thirds)
        lower = inverse_factor(gram_thirds(parts))
        y = dot_thirds(thirds(lower), thirds(z))
    basis = y
    b = thirds(basis)
    left = jnp.concatenate([b[0], b[0], b[1], b[1], b[0], b[2]], axis=0)
    right = jnp.concatenate([b[0], b[1], b[0], b[1], b[2], b[0]], axis=0)
    proj_out[...] = dot(left, right, ((0,), (0,)))
    basis_b = basis.astype(jnp.bfloat16)
    shift = jnp.sum(basis_b.astype(jnp.float32) * mean, axis=1, keepdims=True)
    shift = jnp.broadcast_to(shift, (rank, LANES))
    fetch.wait()
    for g in range(tile_rows // 8):
        for h in range(8 * g, 8 * g + 8):
            s = lax.dot_general(
                basis_b, smooth[h], (((1,), (1,)), ((), ())), preferred_element_type=jnp.float32
            )
            scores[:, h, :] = s - shift
        pltpu.make_async_copy(scores.at[:, pl.ds(8 * g, 8), :], scores_hbm.at[:, pl.ds(8 * g, 8), :], out_sem.at[g]).start()
    for g in range(tile_rows // 8):
        pltpu.make_async_copy(scores.at[:, pl.ds(8 * g, 8), :], scores_hbm.at[:, pl.ds(8 * g, 8), :], out_sem.at[g]).wait()


def components(packed, start, smoothed, count):
    tile_rows, tile_cols, feat = smoothed.shape
    rank = start.shape[1]
    vmem = pl.BlockSpec(memory_space=pltpu.VMEM)
    hbm = pl.BlockSpec(memory_space=pltpu.HBM)
    return pl.pallas_call(
        functools.partial(components_kernel, count),
        out_shape=(
            jax.ShapeDtypeStruct((1, feat), jnp.float32),
            jax.ShapeDtypeStruct((feat, feat), jnp.float32),
            pltpu.HBM((rank, tile_rows, tile_cols), jnp.float32),
        ),
        in_specs=[vmem, vmem, hbm],
        out_specs=(vmem, vmem, hbm),
        scratch_shapes=[
            pltpu.VMEM((feat, feat), jnp.float32),
            pltpu.VMEM((tile_rows, tile_cols, feat), jnp.bfloat16),
            pltpu.VMEM((rank, tile_rows, tile_cols), jnp.float32),
            pltpu.SemaphoreType.DMA,
            pltpu.SemaphoreType.DMA((tile_rows // 8,)),
        ],
        compiler_params=pltpu.CompilerParams(vmem_limit_bytes=40 << 20, flags=FLAGS),
        cost_estimate=pl.CostEstimate(flops=10**9, bytes_accessed=10**7, transcendentals=0),
        name="components",
    )(packed, start, pltpu.with_memory_space_constraint(smoothed, pltpu.HBM))


def local(pixels, start):
    tile_rows, tile_cols, feat = pixels.shape
    rows_total = tile_rows * lax.axis_size("row")
    cols_total = tile_cols * lax.axis_size("col")
    above, below = edges_2(pixels, "row", 0)
    beside = [jnp.concatenate([above[:, c], pixels[:, c], below[:, c]], axis=0) for c in (slice(0, WIDTH), slice(tile_cols - WIDTH, tile_cols))]
    size = lax.axis_size("col")
    left = lax.ppermute(beside[1], "col", [(i, i + 1) for i in range(size - 1)])
    right = lax.ppermute(beside[0], "col", [(i + 1, i) for i in range(size - 1)])
    row_scale = GAUSS[0] / edge_weight(lax.axis_index("row") * tile_rows, tile_rows, rows_total)
    col_scale = 1.0 / edge_weight(lax.axis_index("col") * tile_cols, tile_cols, cols_total)
    col_scale = jnp.broadcast_to(col_scale[:, None], (tile_cols, LANES))
    smoothed, packed = smooth_and_gram(
        pixels, above, below, left, right, column_taps(tile_cols), row_scale, col_scale
    )
    packed = all_sum(packed)
    mean, projector, scores = components(packed, start, smoothed, float(rows_total * cols_total))
    return (mean.reshape(feat), projector, scores)


def solution(mesh):
    in_specs = (P("row", "col", None), P())
    out_specs = (P(), P(), P(None, "row", "col"))
    return jax.shard_map(local, mesh=mesh, in_specs=in_specs, out_specs=out_specs, check_vma=False)
```

```python
import functools

import jax
import jax.numpy as jnp
from jax import lax
from jax.experimental import pallas as pl
from jax.experimental.pallas import tpu as pltpu
from jax.sharding import PartitionSpec as P

ITERS = 4
LANES = 128
AHEAD = 16
CHUNK = 4
FLAGS = {}

GAUSS = (0.0625, 0.25, 0.375, 0.25, 0.0625)


WIDTH = 2
HALO_ROWS = 16


def edges(axis, first, last):
    up = [(i, i + 1) for i in range(lax.axis_size(axis) - 1)]
    down = [(j, i) for i, j in up]
    return lax.ppermute(last, axis, up), lax.ppermute(first, axis, down)


def edge_weight(first, count, total):
    position = first + jnp.arange(count, dtype=jnp.int32)
    weight = jnp.zeros((count,), jnp.float32)
    for offset in range(5):
        inside = (position + offset - 2 >= 0) & (position + offset - 2 < total)
        weight = weight + GAUSS[offset] * inside.astype(jnp.float32)
    return weight


def column_taps(count):
    out = jnp.arange(count, dtype=jnp.int32)[:, None]
    k = jnp.arange(count + HALO_ROWS, dtype=jnp.int32)[None, :]
    beside = k - count
    place = jnp.where(k < count, k, jnp.where(beside < WIDTH, beside - WIDTH, count + beside - WIDTH))
    place = jnp.where(beside < 2 * WIDTH, place, -count)
    taps = jnp.zeros((count, count + HALO_ROWS), jnp.float32)
    for offset in range(5):
        taps = jnp.where(place == out + offset - 2, GAUSS[offset], taps)
    return taps.astype(jnp.bfloat16)


def cascade(c):
    for _ in range(4):
        c = [p + q for p, q in zip(c, c[1:])]
    return c


def correlate(s, gram, ends):
    wide = s.shape[1] - LANES
    over = (((0,), (0,)), ((), ()))
    last = jnp.concatenate([s[:, wide:], jnp.ones((s.shape[0], LANES), jnp.bfloat16)], axis=1)
    gram[...] += lax.dot_general(s[:, :wide], s[:, :wide], over, preferred_element_type=jnp.float32)
    ends[...] += lax.dot_general(s, last, over, preferred_element_type=jnp.float32)


def inner_kernel(
    row_scale, pixels, left, right, taps, col_scale, smooth_hbm, gram, ends,
    source, across, rounded, smooth, in_sem, out_sem,
):
    tile_rows, tile_cols, feat = pixels.shape
    group = 8
    groups = tile_rows // group
    strip = tile_cols // group
    count = lambda g: group if g + 1 < groups else group - 2 * WIDTH

    def fetch(g):
        rows = pl.ds(g * group, group)
        there = source.at[rows, pl.ds(0, tile_cols), :]
        return pltpu.make_async_copy(pixels.at[rows], there, in_sem.at[g])

    def send(g):
        rows = pl.ds(g * group + WIDTH, count(g))
        return pltpu.make_async_copy(smooth.at[rows], smooth_hbm.at[rows], out_sem.at[g])

    for g in range(groups):
        fetch(g).start()
    source[:, tile_cols:, :] = jnp.zeros((tile_rows, HALO_ROWS, feat), jnp.bfloat16)
    source[:, tile_cols : tile_cols + WIDTH, :] = left[...]
    source[:, tile_cols + WIDTH : tile_cols + 2 * WIDTH, :] = right[...]
    gram[...] = jnp.zeros_like(gram)
    ends[...] = jnp.zeros_like(ends)

    def horizontal(g, q):
        across[g % 4, q] = jnp.dot(taps[...], source[group * g + 4 + q], preferred_element_type=jnp.float32)

    def vertical(g, i):
        at = slice(i * strip, (i + 1) * strip)
        scales = [col_scale[at, :] * row_scale[g * group + WIDTH + r] for r in range(count(g))]
        for f in range(feat // LANES):
            lanes = slice(f * LANES, (f + 1) * LANES)
            c = [across[(g - 1) % 4, 4 + r, at, lanes] for r in range(4)]
            c += [across[g % 4, r, at, lanes] for r in range(count(g))]
            for r, total in enumerate(cascade(c)):
                v = (total * scales[r]).astype(jnp.bfloat16)
                smooth[g * group + WIDTH + r, at, lanes] = v
                rounded[g % 2, r, at, lanes] = v

    fetch(0).wait()
    for q in range(4, group):
        horizontal(-1, q)
    fetch(1).wait()
    for q in range(group):
        horizontal(0, q)
    for g in range(groups + 1):
        if g + 2 < groups:
            fetch(g + 2).wait()
        for q in range(group):
            if g + 1 < groups and q < count(g + 1):
                horizontal(g + 1, q)
            if g < groups:
                vertical(g, q)
            if g > 0 and q % CHUNK == CHUNK - 1 and q < count(g - 1):
                rows = rounded[(g - 1) % 2, q - CHUNK + 1 : q + 1]
                correlate(rows.reshape(CHUNK * tile_cols, feat), gram, ends)
        if g < groups:
            send(g).start()
    for g in range(groups):
        send(g).wait()


def edge_kernel(
    row_scale, pixels, above, below, left, right, taps, col_scale, gram_in, ends_in, smooth_in, smooth_hbm, packed,
    source, across, rounded, gram, ends, in_sem, out_sem,
):
    tile_rows, tile_cols, feat = pixels.shape
    own = 2 * WIDTH
    side = own + WIDTH
    starts = (0, tile_rows - own)
    places = (WIDTH, side)
    fetches = [
        pltpu.make_async_copy(
            pixels.at[pl.ds(first, own)], source.at[pl.ds(place, own), pl.ds(0, tile_cols), :], in_sem.at[k]
        )
        for k, (first, place) in enumerate(zip(starts, places))
    ]
    for copy in fetches:
        copy.start()
    source[:, tile_cols:, :] = jnp.zeros((2 * side, HALO_ROWS, feat), jnp.bfloat16)
    source[0:WIDTH, 0 : tile_cols + 2 * WIDTH, :] = above[...]
    source[side + own :, 0 : tile_cols + 2 * WIDTH, :] = below[...]
    for first, place in zip(starts, places):
        rows, there = (slice(first, first + own), slice(place, place + own))
        source[there, tile_cols : tile_cols + WIDTH, :] = left[rows]
        source[there, tile_cols + WIDTH : tile_cols + 2 * WIDTH, :] = right[rows]
    for copy in fetches:
        copy.wait()
    for k in range(2 * side):
        across[k] = jnp.dot(taps[...], source[k], preferred_element_type=jnp.float32)
    sends = []
    strip = 16
    for k, first in enumerate((0, tile_rows - WIDTH)):
        for i in range(tile_cols // strip):
            at = slice(i * strip, (i + 1) * strip)
            scales = [col_scale[at, :] * row_scale[first + r] for r in range(WIDTH)]
            for f in range(feat // LANES):
                lanes = slice(f * LANES, (f + 1) * LANES)
                c = [across[side * k + r, at, lanes] for r in range(side)]
                for r, total in enumerate(cascade(c)):
                    rounded[WIDTH * k + r, at, lanes] = (total * scales[r]).astype(jnp.bfloat16)
        sends.append(
            pltpu.make_async_copy(
                rounded.at[pl.ds(WIDTH * k, WIDTH)], smooth_hbm.at[pl.ds(first, WIDTH)], out_sem.at[k]
            )
        )
        sends[-1].start()
    gram[...] = gram_in[...]
    ends[...] = ends_in[...]
    correlate(rounded[...].reshape(2 * WIDTH * tile_cols, feat), gram, ends)
    row = lax.broadcasted_iota(jnp.int32, (LANES, LANES), 0)
    col = lax.broadcasted_iota(jnp.int32, (LANES, LANES), 1)
    n = feat // LANES
    at = 0
    for i in range(n):
        for j in range(i, n):
            rows = slice(i * LANES, (i + 1) * LANES)
            block = ends[rows, :LANES] if j == n - 1 else gram[rows, j * LANES : (j + 1) * LANES]
            if i == j:
                piece = ends[rows, LANES:]
                block = jnp.where((col == 0) & (row > 0), piece, block)
                block = jnp.where((col == 1) & (row == LANES - 1), piece[0:1, :], block)
            packed[at * LANES : (at + 1) * LANES, :] = block
            at += 1
    for copy in sends:
        copy.wait()


def smooth_and_gram(pixels, left, right, row_edges, taps, row_scale, col_scale):
    tile_rows, tile_cols, feat = pixels.shape
    n = feat // LANES
    wide = feat - LANES
    vmem = pl.BlockSpec(memory_space=pltpu.VMEM)
    hbm = pl.BlockSpec(memory_space=pltpu.HBM)
    smem = pl.BlockSpec(memory_space=pltpu.SMEM)
    pixels = pltpu.with_memory_space_constraint(pixels, pltpu.HBM)
    above, below = row_edges
    width = tile_cols + HALO_ROWS
    smoothed, gram, ends = pl.pallas_call(
        inner_kernel,
        out_shape=(
            pltpu.HBM(pixels.shape, jnp.bfloat16),
            jax.ShapeDtypeStruct((wide, wide), jnp.float32),
            jax.ShapeDtypeStruct((feat, 2 * LANES), jnp.float32),
        ),
        in_specs=[smem, hbm, vmem, vmem, vmem, vmem],
        out_specs=(hbm, vmem, vmem),
        scratch_shapes=[
            pltpu.VMEM((tile_rows, width, feat), jnp.bfloat16),
            pltpu.VMEM((4, 8, tile_cols, feat), jnp.float32),
            pltpu.VMEM((2, 8, tile_cols, feat), jnp.bfloat16),
            pltpu.VMEM(pixels.shape, jnp.bfloat16),
            pltpu.SemaphoreType.DMA((tile_rows // 8,)),
            pltpu.SemaphoreType.DMA((tile_rows // 8,)),
        ],
        compiler_params=pltpu.CompilerParams(vmem_limit_bytes=40 << 20, flags=FLAGS),
        cost_estimate=pl.CostEstimate(flops=10**10, bytes_accessed=3 * 10**7, transcendentals=0),
        name="smooth_inner",
    )(row_scale, pixels, left, right, taps, col_scale)
    smoothed = pltpu.with_memory_space_constraint(smoothed, pltpu.HBM)
    side = 3 * WIDTH
    return pl.pallas_call(
        edge_kernel,
        out_shape=(
            pltpu.HBM(pixels.shape, jnp.bfloat16),
            jax.ShapeDtypeStruct((n * (n + 1) // 2 * LANES, LANES), jnp.float32),
        ),
        in_specs=[smem, hbm] + [vmem] * 8 + [hbm],
        out_specs=(hbm, vmem),
        input_output_aliases={10: 0},
        scratch_shapes=[
            pltpu.VMEM((2 * side, width, feat), jnp.bfloat16),
            pltpu.VMEM((2 * side, tile_cols, feat), jnp.float32),
            pltpu.VMEM((2 * WIDTH, tile_cols, feat), jnp.bfloat16),
            pltpu.VMEM((wide, wide), jnp.float32),
            pltpu.VMEM((feat, 2 * LANES), jnp.float32),
            pltpu.SemaphoreType.DMA((2,)),
            pltpu.SemaphoreType.DMA((2,)),
        ],
        compiler_params=pltpu.CompilerParams(vmem_limit_bytes=40 << 20),
        cost_estimate=pl.CostEstimate(flops=10**9, bytes_accessed=10**6, transcendentals=0),
        name="smooth_edges",
    )(row_scale, pixels, above, below, left, right, taps, col_scale, gram, ends, smoothed)


def all_sum(values):
    axes = ("row", "col")
    rows, cols = lax.axis_size("row"), lax.axis_size("col")
    if rows & (rows - 1) or cols & (cols - 1) or cols < 2:
        return lax.psum(values, axes)

    def pairs(row_bit, col_bit):
        return [(r * cols + c, (r ^ row_bit) * cols + (c ^ col_bit)) for r in range(rows) for c in range(cols)]

    core = pairs(0, 1)
    odd = lax.axis_index("col") % 2
    half = values.shape[0] // 2
    mine = lax.dynamic_slice_in_dim(values, odd * half, half)
    other = lax.dynamic_slice_in_dim(values, (1 - odd) * half, half)
    kept = mine + lax.ppermute(other, axes, core)
    row_steps = [pairs(1 << k, 0) for k in range(rows.bit_length() - 1)]
    col_steps = [pairs(0, 1 << k) for k in range(1, cols.bit_length() - 1)]
    order = row_steps[:1] + col_steps + row_steps[1:]
    swapped = list(order)
    for k in range(0, len(order) - 1, 2):
        swapped[k], swapped[k + 1] = order[k + 1], order[k]
    quarter = half // 2
    a, b = kept[:quarter], kept[quarter:]
    for first, second in zip(order, swapped):
        got_a = lax.ppermute(a, axes, first)
        got_b = lax.ppermute(b, axes, second)
        a = a + got_a
        b = b + got_b
    kept = jnp.concatenate([a, b])
    got = lax.ppermute(kept, axes, core)
    return jnp.where(odd == 0, jnp.concatenate([kept, got]), jnp.concatenate([got, kept]))


def inverse_factor(a):
    n = a.shape[0]
    row = lax.broadcasted_iota(jnp.int32, (n, n), 0)
    col = lax.broadcasted_iota(jnp.int32, (n, n), 1)
    work = jnp.concatenate([a, (row == col).astype(jnp.float32)], axis=1)
    blocks = [work[8 * i : 8 * i + 8] for i in range(n // 8)]
    sub = lax.broadcasted_iota(jnp.int32, (8, 2 * n), 0)
    ahead = min(AHEAD, n)
    pivots = []
    for j0 in range(0, n, ahead):
        first = j0 // 8
        cols = [
            {i: jnp.broadcast_to(blocks[i][:, j : j + 1], (8, 2 * n)) for i in range(j // 8, n // 8)}
            for j in range(j0, j0 + ahead)
        ]
        for k in range(ahead):
            j = j0 + k
            top = j // 8
            s = j - 8 * top
            recip = 1.0 / jnp.broadcast_to(cols[k][top][s : s + 1], (8, 2 * n))
            pivots.append(recip)
            factor = dict(cols[k])
            factor[top] = jnp.where(sub > s, factor[top], 0.0)
            for m in range(k + 1, ahead):
                other = (j0 + m) // 8
                t = j0 + m - 8 * other
                scaled = jnp.broadcast_to(cols[k][other][t : t + 1], (8, 2 * n)) * recip
                for i in cols[m]:
                    cols[m][i] = cols[m][i] - factor[i] * scaled
            line = jnp.broadcast_to(blocks[top][s : s + 1], (8, 2 * n)) * recip
            for i in range(top, n // 8):
                blocks[i] = blocks[i] - factor[i] * line
    out = []
    for i in range(n // 8):
        scale = pivots[8 * i]
        for s in range(1, 8):
            scale = jnp.where(sub == s, pivots[8 * i + s], scale)
        out.append((blocks[i] * lax.sqrt(scale))[:, n:])
    return jnp.concatenate(out, axis=0)


def thirds(x):
    high = x.astype(jnp.bfloat16)
    rest = x - high.astype(jnp.float32)
    middle = rest.astype(jnp.bfloat16)
    return high, middle, (rest - middle.astype(jnp.float32)).astype(jnp.bfloat16)


def dot(a, b, contract):
    return lax.dot_general(a, b, (contract, ((), ())), preferred_element_type=jnp.float32)


def dot_thirds(a, b):
    m = a[0].shape[0]
    one = dot(jnp.concatenate(a, axis=0), b[0], ((1,), (0,)))
    two = dot(jnp.concatenate(a[:2], axis=0), b[1], ((1,), (0,)))
    low = one[2 * m :] + two[m:] + dot(a[0], b[2], ((1,), (0,)))
    return one[:m] + (one[m : 2 * m] + two[:m] + low)


def gram_thirds(y):
    m = y[0].shape[0]
    stack = jnp.concatenate(y, axis=0)
    p = dot(stack, stack, ((1,), (1,)))
    part = lambda i, j: p[i * m : (i + 1) * m, j * m : (j + 1) * m]
    return part(0, 0) + ((part(0, 1) + part(1, 0)) + (part(1, 1) + (part(0, 2) + part(2, 0))))


def components_kernel(count, packed, start, smooth_hbm, mean_out, proj_out, scores_hbm, cov, smooth, scores, in_sem, out_sem):
    feat = cov.shape[0]
    n = feat // LANES
    rank = start.shape[1]
    tile_rows = smooth.shape[0]
    fetch = pltpu.make_async_copy(smooth_hbm, smooth, in_sem)
    fetch.start()
    row = lax.broadcasted_iota(jnp.int32, (LANES, LANES), 0)
    col = lax.broadcasted_iota(jnp.int32, (LANES, LANES), 1)
    inv = 1.0 / count
    index = {}
    for i in range(n):
        for j in range(i, n):
            index[i, j] = len(index)
    block = lambda i, j: packed[index[i, j] * LANES : (index[i, j] + 1) * LANES, :]
    means, mean_cols, diag = [], [], []
    for i in range(n):
        b = block(i, i)
        bt = b.T
        first = jnp.broadcast_to(b[LANES - 1 : LANES, 1:2], (LANES, LANES))
        m = jnp.where(row > 0, jnp.broadcast_to(b[:, 0:1], (LANES, LANES)), first) * inv
        means.append(m.T[0:1, :])
        mean_cols.append(m)
        diag.append(jnp.where(row <= col, b, bt))
    mean = jnp.concatenate(means, axis=1)
    mean_out[...] = mean
    for i in range(n):
        for j in range(i, n):
            g = diag[i] if i == j else block(i, j)
            c = g * inv - mean_cols[i] * means[j]
            cov[i * LANES : (i + 1) * LANES, j * LANES : (j + 1) * LANES] = c
            if i != j:
                cov[j * LANES : (j + 1) * LANES, i * LANES : (i + 1) * LANES] = c.T
    cov_thirds = thirds(cov[...])
    y = dot_thirds(thirds(start[...].T), cov_thirds)
    for step in range(ITERS):
        parts = thirds(y)
        z = y if step == ITERS - 1 else dot_thirds(parts, cov_thirds)
        lower = inverse_factor(gram_thirds(parts))
        y = dot_thirds(thirds(lower), thirds(z))
    basis = y
    b = thirds(basis)
    left = jnp.concatenate([b[0], b[0], b[1], b[1], b[0], b[2]], axis=0)
    right = jnp.concatenate([b[0], b[1], b[0], b[1], b[2], b[0]], axis=0)
    proj_out[...] = dot(left, right, ((0,), (0,)))
    basis_b = basis.astype(jnp.bfloat16)
    shift = jnp.sum(basis_b.astype(jnp.float32) * mean, axis=1, keepdims=True)
    shift = jnp.broadcast_to(shift, (rank, LANES))
    fetch.wait()
    for g in range(tile_rows // 8):
        for h in range(8 * g, 8 * g + 8):
            s = lax.dot_general(
                basis_b, smooth[h], (((1,), (1,)), ((), ())), preferred_element_type=jnp.float32
            )
            scores[:, h, :] = s - shift
        pltpu.make_async_copy(scores.at[:, pl.ds(8 * g, 8), :], scores_hbm.at[:, pl.ds(8 * g, 8), :], out_sem.at[g]).start()
    for g in range(tile_rows // 8):
        pltpu.make_async_copy(scores.at[:, pl.ds(8 * g, 8), :], scores_hbm.at[:, pl.ds(8 * g, 8), :], out_sem.at[g]).wait()


def components(packed, start, smoothed, count):
    tile_rows, tile_cols, feat = smoothed.shape
    rank = start.shape[1]
    vmem = pl.BlockSpec(memory_space=pltpu.VMEM)
    hbm = pl.BlockSpec(memory_space=pltpu.HBM)
    return pl.pallas_call(
        functools.partial(components_kernel, count),
        out_shape=(
            jax.ShapeDtypeStruct((1, feat), jnp.float32),
            jax.ShapeDtypeStruct((feat, feat), jnp.float32),
            pltpu.HBM((rank, tile_rows, tile_cols), jnp.float32),
        ),
        in_specs=[vmem, vmem, hbm],
        out_specs=(vmem, vmem, hbm),
        scratch_shapes=[
            pltpu.VMEM((feat, feat), jnp.float32),
            pltpu.VMEM((tile_rows, tile_cols, feat), jnp.bfloat16),
            pltpu.VMEM((rank, tile_rows, tile_cols), jnp.float32),
            pltpu.SemaphoreType.DMA,
            pltpu.SemaphoreType.DMA((tile_rows // 8,)),
        ],
        compiler_params=pltpu.CompilerParams(vmem_limit_bytes=40 << 20, flags=FLAGS),
        cost_estimate=pl.CostEstimate(flops=10**9, bytes_accessed=10**7, transcendentals=0),
        name="components",
    )(packed, start, pltpu.with_memory_space_constraint(smoothed, pltpu.HBM))


def local(pixels, start):
    tile_rows, tile_cols, feat = pixels.shape
    rows_total = tile_rows * lax.axis_size("row")
    cols_total = tile_cols * lax.axis_size("col")
    left, right = edges("col", pixels[:, :WIDTH], pixels[:, tile_cols - WIDTH :])
    wider = lambda rows: jnp.concatenate([pixels[rows], left[rows], right[rows]], axis=1)
    row_edges = edges("row", wider(slice(0, WIDTH)), wider(slice(tile_rows - WIDTH, tile_rows)))
    row_scale = GAUSS[0] / edge_weight(lax.axis_index("row") * tile_rows, tile_rows, rows_total)
    col_scale = 1.0 / edge_weight(lax.axis_index("col") * tile_cols, tile_cols, cols_total)
    col_scale = jnp.broadcast_to(col_scale[:, None], (tile_cols, LANES))
    smoothed, packed = smooth_and_gram(
        pixels, left, right, row_edges, column_taps(tile_cols), row_scale, col_scale
    )
    packed = all_sum(packed)
    mean, projector, scores = components(packed, start, smoothed, float(rows_total * cols_total))
    return (mean.reshape(feat), projector, scores)


def solution(mesh):
    in_specs = (P("row", "col", None), P())
    out_specs = (P(), P(), P(None, "row", "col"))
    return jax.shard_map(local, mesh=mesh, in_specs=in_specs, out_specs=out_specs, check_vma=False)
```

```python
import functools

import jax
import jax.numpy as jnp
from jax import lax
from jax.experimental import pallas as pl
from jax.experimental.pallas import tpu as pltpu
from jax.sharding import PartitionSpec as P

ITERS = 4
LANES = 128
AHEAD = 16
CHUNK = 4
FLAGS = {}

GAUSS = (0.0625, 0.25, 0.375, 0.25, 0.0625)


WIDTH = 2
HALO_ROWS = 16


def edges(axis, first, last):
    up = [(i, i + 1) for i in range(lax.axis_size(axis) - 1)]
    down = [(j, i) for i, j in up]
    return lax.ppermute(last, axis, up), lax.ppermute(first, axis, down)


def edge_weight(first, count, total):
    position = first + jnp.arange(count, dtype=jnp.int32)
    weight = jnp.zeros((count,), jnp.float32)
    for offset in range(5):
        inside = (position + offset - 2 >= 0) & (position + offset - 2 < total)
        weight = weight + GAUSS[offset] * inside.astype(jnp.float32)
    return weight


def column_taps(count):
    out = jnp.arange(count, dtype=jnp.int32)[:, None]
    k = jnp.arange(count + HALO_ROWS, dtype=jnp.int32)[None, :]
    beside = k - count
    place = jnp.where(k < count, k, jnp.where(beside < WIDTH, beside - WIDTH, count + beside - WIDTH))
    place = jnp.where(beside < 2 * WIDTH, place, -count)
    taps = jnp.zeros((count, count + HALO_ROWS), jnp.float32)
    for offset in range(5):
        taps = jnp.where(place == out + offset - 2, GAUSS[offset], taps)
    return taps.astype(jnp.bfloat16)


def cascade(c):
    for _ in range(4):
        c = [p + q for p, q in zip(c, c[1:])]
    return c


def correlate(s, gram, ends):
    wide = s.shape[1] - LANES
    over = (((0,), (0,)), ((), ()))
    last = jnp.concatenate([s[:, wide:], jnp.ones((s.shape[0], LANES), jnp.bfloat16)], axis=1)
    gram[...] += lax.dot_general(s[:, :wide], s[:, :wide], over, preferred_element_type=jnp.float32)
    ends[...] += lax.dot_general(s, last, over, preferred_element_type=jnp.float32)


def inner_kernel(
    row_scale, pixels, left, right, taps, col_scale, smooth_hbm, gram, ends,
    source, across, rounded, smooth, in_sem, out_sem,
):
    tile_rows, tile_cols, feat = pixels.shape
    group = 8
    groups = tile_rows // group
    strip = tile_cols // group
    count = lambda g: group if g + 1 < groups else group - 2 * WIDTH

    def fetch(g):
        rows = pl.ds(g * group, group)
        there = source.at[rows, pl.ds(0, tile_cols), :]
        return pltpu.make_async_copy(pixels.at[rows], there, in_sem.at[g])

    def send(g):
        rows = pl.ds(g * group + WIDTH, count(g))
        return pltpu.make_async_copy(smooth.at[rows], smooth_hbm.at[rows], out_sem.at[g])

    for g in range(groups):
        fetch(g).start()
    source[:, tile_cols:, :] = jnp.zeros((tile_rows, HALO_ROWS, feat), jnp.bfloat16)
    source[:, tile_cols : tile_cols + WIDTH, :] = left[...]
    source[:, tile_cols + WIDTH : tile_cols + 2 * WIDTH, :] = right[...]
    gram[...] = jnp.zeros_like(gram)
    ends[...] = jnp.zeros_like(ends)

    def horizontal(g, q):
        across[g % 4, q] = jnp.dot(taps[...], source[group * g + 4 + q], preferred_element_type=jnp.float32)

    def vertical(g, i):
        at = slice(i * strip, (i + 1) * strip)
        scales = [col_scale[at, :] * row_scale[g * group + WIDTH + r] for r in range(count(g))]
        for f in range(feat // LANES):
            lanes = slice(f * LANES, (f + 1) * LANES)
            c = [across[(g - 1) % 4, 4 + r, at, lanes] for r in range(4)]
            c += [across[g % 4, r, at, lanes] for r in range(count(g))]
            for r, total in enumerate(cascade(c)):
                v = (total * scales[r]).astype(jnp.bfloat16)
                smooth[g * group + WIDTH + r, at, lanes] = v
                rounded[g % 2, r, at, lanes] = v

    fetch(0).wait()
    for q in range(4, group):
        horizontal(-1, q)
    fetch(1).wait()
    for q in range(group):
        horizontal(0, q)
    for g in range(groups + 1):
        if g + 2 < groups:
            fetch(g + 2).wait()
        for q in range(group):
            if g + 1 < groups and q < count(g + 1):
                horizontal(g + 1, q)
            if g < groups:
                vertical(g, q)
            if g > 0 and q % CHUNK == CHUNK - 1 and q < count(g - 1):
                rows = rounded[(g - 1) % 2, q - CHUNK + 1 : q + 1]
                correlate(rows.reshape(CHUNK * tile_cols, feat), gram, ends)
        if g < groups:
            send(g).start()
    for g in range(groups):
        send(g).wait()


def edge_kernel(
    row_scale, pixels, above, below, left, right, taps, col_scale, gram_in, ends_in, smooth_in, smooth_hbm, packed,
    source, across, rounded, gram, ends, in_sem, out_sem,
):
    tile_rows, tile_cols, feat = pixels.shape
    own = 2 * WIDTH
    side = own + WIDTH
    starts = (0, tile_rows - own)
    places = (WIDTH, side)
    fetches = [
        pltpu.make_async_copy(
            pixels.at[pl.ds(first, own)], source.at[pl.ds(place, own), pl.ds(0, tile_cols), :], in_sem.at[k]
        )
        for k, (first, place) in enumerate(zip(starts, places))
    ]
    for copy in fetches:
        copy.start()
    source[:, tile_cols:, :] = jnp.zeros((2 * side, HALO_ROWS, feat), jnp.bfloat16)
    source[0:WIDTH, 0 : tile_cols + 2 * WIDTH, :] = above[...]
    source[side + own :, 0 : tile_cols + 2 * WIDTH, :] = below[...]
    for first, place in zip(starts, places):
        rows, there = (slice(first, first + own), slice(place, place + own))
        source[there, tile_cols : tile_cols + WIDTH, :] = left[rows]
        source[there, tile_cols + WIDTH : tile_cols + 2 * WIDTH, :] = right[rows]
    for copy in fetches:
        copy.wait()
    for k in range(2 * side):
        across[k] = jnp.dot(taps[...], source[k], preferred_element_type=jnp.float32)
    sends = []
    strip = 16
    for k, first in enumerate((0, tile_rows - WIDTH)):
        for i in range(tile_cols // strip):
            at = slice(i * strip, (i + 1) * strip)
            scales = [col_scale[at, :] * row_scale[first + r] for r in range(WIDTH)]
            for f in range(feat // LANES):
                lanes = slice(f * LANES, (f + 1) * LANES)
                c = [across[side * k + r, at, lanes] for r in range(side)]
                for r, total in enumerate(cascade(c)):
                    rounded[WIDTH * k + r, at, lanes] = (total * scales[r]).astype(jnp.bfloat16)
        sends.append(
            pltpu.make_async_copy(
                rounded.at[pl.ds(WIDTH * k, WIDTH)], smooth_hbm.at[pl.ds(first, WIDTH)], out_sem.at[k]
            )
        )
        sends[-1].start()
    gram[...] = gram_in[...]
    ends[...] = ends_in[...]
    correlate(rounded[...].reshape(2 * WIDTH * tile_cols, feat), gram, ends)
    row = lax.broadcasted_iota(jnp.int32, (LANES, LANES), 0)
    col = lax.broadcasted_iota(jnp.int32, (LANES, LANES), 1)
    n = feat // LANES
    at = 0
    for i in range(n):
        for j in range(i, n):
            rows = slice(i * LANES, (i + 1) * LANES)
            block = ends[rows, :LANES] if j == n - 1 else gram[rows, j * LANES : (j + 1) * LANES]
            if i == j:
                piece = ends[rows, LANES:]
                block = jnp.where((col == 0) & (row > 0), piece, block)
                block = jnp.where((col == 1) & (row == LANES - 1), piece[0:1, :], block)
            packed[at * LANES : (at + 1) * LANES, :] = block
            at += 1
    for copy in sends:
        copy.wait()


def smooth_and_gram(pixels, left, right, row_edges, taps, row_scale, col_scale):
    tile_rows, tile_cols, feat = pixels.shape
    n = feat // LANES
    wide = feat - LANES
    vmem = pl.BlockSpec(memory_space=pltpu.VMEM)
    hbm = pl.BlockSpec(memory_space=pltpu.HBM)
    smem = pl.BlockSpec(memory_space=pltpu.SMEM)
    pixels = pltpu.with_memory_space_constraint(pixels, pltpu.HBM)
    above, below = row_edges
    width = tile_cols + HALO_ROWS
    smoothed, gram, ends = pl.pallas_call(
        inner_kernel,
        out_shape=(
            pltpu.HBM(pixels.shape, jnp.bfloat16),
            jax.ShapeDtypeStruct((wide, wide), jnp.float32),
            jax.ShapeDtypeStruct((feat, 2 * LANES), jnp.float32),
        ),
        in_specs=[smem, hbm, vmem, vmem, vmem, vmem],
        out_specs=(hbm, vmem, vmem),
        scratch_shapes=[
            pltpu.VMEM((tile_rows, width, feat), jnp.bfloat16),
            pltpu.VMEM((4, 8, tile_cols, feat), jnp.float32),
            pltpu.VMEM((2, 8, tile_cols, feat), jnp.bfloat16),
            pltpu.VMEM(pixels.shape, jnp.bfloat16),
            pltpu.SemaphoreType.DMA((tile_rows // 8,)),
            pltpu.SemaphoreType.DMA((tile_rows // 8,)),
        ],
        compiler_params=pltpu.CompilerParams(vmem_limit_bytes=40 << 20, flags=FLAGS),
        cost_estimate=pl.CostEstimate(flops=10**10, bytes_accessed=3 * 10**7, transcendentals=0),
        name="smooth_inner",
    )(row_scale, pixels, left, right, taps, col_scale)
    smoothed = pltpu.with_memory_space_constraint(smoothed, pltpu.HBM)
    side = 3 * WIDTH
    return pl.pallas_call(
        edge_kernel,
        out_shape=(
            pltpu.HBM(pixels.shape, jnp.bfloat16),
            jax.ShapeDtypeStruct((n * (n + 1) // 2 * LANES, LANES), jnp.float32),
        ),
        in_specs=[smem, hbm] + [vmem] * 8 + [hbm],
        out_specs=(hbm, vmem),
        input_output_aliases={10: 0},
        scratch_shapes=[
            pltpu.VMEM((2 * side, width, feat), jnp.bfloat16),
            pltpu.VMEM((2 * side, tile_cols, feat), jnp.float32),
            pltpu.VMEM((2 * WIDTH, tile_cols, feat), jnp.bfloat16),
            pltpu.VMEM((wide, wide), jnp.float32),
            pltpu.VMEM((feat, 2 * LANES), jnp.float32),
            pltpu.SemaphoreType.DMA((2,)),
            pltpu.SemaphoreType.DMA((2,)),
        ],
        compiler_params=pltpu.CompilerParams(vmem_limit_bytes=40 << 20),
        cost_estimate=pl.CostEstimate(flops=10**9, bytes_accessed=10**6, transcendentals=0),
        name="smooth_edges",
    )(row_scale, pixels, above, below, left, right, taps, col_scale, gram, ends, smoothed)


def all_sum(values):
    axes = ("row", "col")
    rows, cols = lax.axis_size("row"), lax.axis_size("col")
    if rows & (rows - 1) or cols & (cols - 1) or cols < 2:
        return lax.psum(values, axes)

    def pairs(row_bit, col_bit):
        return [(r * cols + c, (r ^ row_bit) * cols + (c ^ col_bit)) for r in range(rows) for c in range(cols)]

    core = pairs(0, 1)
    odd = lax.axis_index("col") % 2
    half = values.shape[0] // 2
    mine = lax.dynamic_slice_in_dim(values, odd * half, half)
    other = lax.dynamic_slice_in_dim(values, (1 - odd) * half, half)
    kept = mine + lax.ppermute(other, axes, core)
    row_steps = [pairs(1 << k, 0) for k in range(rows.bit_length() - 1)]
    col_steps = [pairs(0, 1 << k) for k in range(1, cols.bit_length() - 1)]
    order = row_steps[:1] + col_steps + row_steps[1:]
    turned = order[len(order) // 2 :] + order[: len(order) // 2]
    quarter = half // 2
    a, b = kept[:quarter], kept[quarter:]
    for first, second in zip(order, turned):
        got_a = lax.ppermute(a, axes, first)
        got_b = lax.ppermute(b, axes, second)
        a = a + got_a
        b = b + got_b
    kept = jnp.concatenate([a, b])
    got = lax.ppermute(kept, axes, core)
    return jnp.where(odd == 0, jnp.concatenate([kept, got]), jnp.concatenate([got, kept]))


def inverse_factor(a):
    n = a.shape[0]
    row = lax.broadcasted_iota(jnp.int32, (n, n), 0)
    col = lax.broadcasted_iota(jnp.int32, (n, n), 1)
    work = jnp.concatenate([a, (row == col).astype(jnp.float32)], axis=1)
    blocks = [work[8 * i : 8 * i + 8] for i in range(n // 8)]
    sub = lax.broadcasted_iota(jnp.int32, (8, 2 * n), 0)
    ahead = min(AHEAD, n)
    pivots = []
    for j0 in range(0, n, ahead):
        first = j0 // 8
        cols = [
            {i: jnp.broadcast_to(blocks[i][:, j : j + 1], (8, 2 * n)) for i in range(j // 8, n // 8)}
            for j in range(j0, j0 + ahead)
        ]
        for k in range(ahead):
            j = j0 + k
            top = j // 8
            s = j - 8 * top
            recip = 1.0 / jnp.broadcast_to(cols[k][top][s : s + 1], (8, 2 * n))
            pivots.append(recip)
            factor = dict(cols[k])
            factor[top] = jnp.where(sub > s, factor[top], 0.0)
            for m in range(k + 1, ahead):
                other = (j0 + m) // 8
                t = j0 + m - 8 * other
                scaled = jnp.broadcast_to(cols[k][other][t : t + 1], (8, 2 * n)) * recip
                for i in cols[m]:
                    cols[m][i] = cols[m][i] - factor[i] * scaled
            line = jnp.broadcast_to(blocks[top][s : s + 1], (8, 2 * n)) * recip
            for i in range(top, n // 8):
                blocks[i] = blocks[i] - factor[i] * line
    out = []
    for i in range(n // 8):
        scale = pivots[8 * i]
        for s in range(1, 8):
            scale = jnp.where(sub == s, pivots[8 * i + s], scale)
        out.append((blocks[i] * lax.sqrt(scale))[:, n:])
    return jnp.concatenate(out, axis=0)


def thirds(x):
    high = x.astype(jnp.bfloat16)
    rest = x - high.astype(jnp.float32)
    middle = rest.astype(jnp.bfloat16)
    return high, middle, (rest - middle.astype(jnp.float32)).astype(jnp.bfloat16)


def dot(a, b, contract):
    return lax.dot_general(a, b, (contract, ((), ())), preferred_element_type=jnp.float32)


def dot_thirds(a, b):
    m = a[0].shape[0]
    one = dot(jnp.concatenate(a, axis=0), b[0], ((1,), (0,)))
    two = dot(jnp.concatenate(a[:2], axis=0), b[1], ((1,), (0,)))
    low = one[2 * m :] + two[m:] + dot(a[0], b[2], ((1,), (0,)))
    return one[:m] + (one[m : 2 * m] + two[:m] + low)


def gram_thirds(y):
    m = y[0].shape[0]
    stack = jnp.concatenate(y, axis=0)
    p = dot(stack, stack, ((1,), (1,)))
    part = lambda i, j: p[i * m : (i + 1) * m, j * m : (j + 1) * m]
    return part(0, 0) + ((part(0, 1) + part(1, 0)) + (part(1, 1) + (part(0, 2) + part(2, 0))))


def components_kernel(
    count, packed, start, smooth_hbm, mean_out, proj_out, scores_hbm,
    cov, cov_thirds, subspace, basis_b, shift, smooth, scores, in_sem, out_sem,
):
    feat = cov.shape[0]
    n = feat // LANES
    rank = start.shape[1]
    tile_rows = smooth.shape[0]
    fetch = pltpu.make_async_copy(smooth_hbm, smooth, in_sem)
    fetch.start()
    row = lax.broadcasted_iota(jnp.int32, (LANES, LANES), 0)
    col = lax.broadcasted_iota(jnp.int32, (LANES, LANES), 1)
    inv = 1.0 / count
    index = {}
    for i in range(n):
        for j in range(i, n):
            index[i, j] = len(index)
    block = lambda i, j: packed[index[i, j] * LANES : (index[i, j] + 1) * LANES, :]
    means, mean_cols, diag = [], [], []
    for i in range(n):
        b = block(i, i)
        bt = b.T
        first = jnp.broadcast_to(b[LANES - 1 : LANES, 1:2], (LANES, LANES))
        m = jnp.where(row > 0, jnp.broadcast_to(b[:, 0:1], (LANES, LANES)), first) * inv
        means.append(m.T[0:1, :])
        mean_cols.append(m)
        diag.append(jnp.where(row <= col, b, bt))
    mean = jnp.concatenate(means, axis=1)
    mean_out[...] = mean[0]
    for i in range(n):
        for j in range(i, n):
            g = diag[i] if i == j else block(i, j)
            c = g * inv - mean_cols[i] * means[j]
            cov[i * LANES : (i + 1) * LANES, j * LANES : (j + 1) * LANES] = c
            if i != j:
                cov[j * LANES : (j + 1) * LANES, i * LANES : (i + 1) * LANES] = c.T
    split = thirds(cov[...])
    for k in range(3):
        cov_thirds[k] = split[k]
    product = lambda parts: dot_thirds(parts, [cov_thirds[k] for k in range(3)])
    subspace[...] = product(thirds(start[...].T))

    @pl.loop(0, ITERS - 1)
    def _(step):
        parts = thirds(subspace[...])
        z = product(parts)
        lower = inverse_factor(gram_thirds(parts))
        subspace[...] = dot_thirds(thirds(lower), thirds(z))

    parts = thirds(subspace[...])
    lower = inverse_factor(gram_thirds(parts))
    y = dot_thirds(thirds(lower), parts)
    basis = y
    b = thirds(basis)
    left = jnp.concatenate([b[0], b[0], b[1], b[1], b[0], b[2]], axis=0)
    right = jnp.concatenate([b[0], b[1], b[0], b[1], b[2], b[0]], axis=0)
    proj_out[...] = dot(left, right, ((0,), (0,)))
    rounded = basis.astype(jnp.bfloat16)
    basis_b[...] = rounded
    total = jnp.sum(rounded.astype(jnp.float32) * mean, axis=1, keepdims=True)
    shift[...] = jnp.broadcast_to(total, (rank, LANES))
    fetch.wait()

    def send(g):
        here = scores.at[g].reshape(rank, 8, smooth.shape[1])
        return pltpu.make_async_copy(here, scores_hbm.at[:, pl.ds(8 * g, 8), :], out_sem.at[g])

    groups = tile_rows // 8

    @pl.loop(0, groups, unroll=2)
    def _(g):
        for h in range(8):
            s = dot(basis_b[...], smooth[8 * g + h], ((1,), (1,)))
            scores[g, pl.ds(h, rank, stride=8), :] = s - shift[...]
        send(g).start()

    for g in range(groups):
        send(g).wait()


def components(packed, start, smoothed, count):
    tile_rows, tile_cols, feat = smoothed.shape
    rank = start.shape[1]
    vmem = pl.BlockSpec(memory_space=pltpu.VMEM)
    hbm = pl.BlockSpec(memory_space=pltpu.HBM)
    return pl.pallas_call(
        functools.partial(components_kernel, count),
        out_shape=(
            jax.ShapeDtypeStruct((feat,), jnp.float32),
            jax.ShapeDtypeStruct((feat, feat), jnp.float32),
            pltpu.HBM((rank, tile_rows, tile_cols), jnp.float32),
        ),
        in_specs=[vmem, vmem, hbm],
        out_specs=(vmem, vmem, hbm),
        scratch_shapes=[
            pltpu.VMEM((feat, feat), jnp.float32),
            pltpu.VMEM((3, feat, feat), jnp.bfloat16),
            pltpu.VMEM((rank, feat), jnp.float32),
            pltpu.VMEM((rank, feat), jnp.bfloat16),
            pltpu.VMEM((rank, LANES), jnp.float32),
            pltpu.VMEM((tile_rows, tile_cols, feat), jnp.bfloat16),
            pltpu.VMEM((tile_rows // 8, rank * 8, tile_cols), jnp.float32),
            pltpu.SemaphoreType.DMA,
            pltpu.SemaphoreType.DMA((tile_rows // 8,)),
        ],
        compiler_params=pltpu.CompilerParams(vmem_limit_bytes=40 << 20, flags=FLAGS),
        cost_estimate=pl.CostEstimate(flops=10**9, bytes_accessed=10**7, transcendentals=0),
        name="components",
    )(packed, start, pltpu.with_memory_space_constraint(smoothed, pltpu.HBM))


def local(pixels, start):
    tile_rows, tile_cols, feat = pixels.shape
    rows_total = tile_rows * lax.axis_size("row")
    cols_total = tile_cols * lax.axis_size("col")
    left, right = edges("col", pixels[:, :WIDTH], pixels[:, tile_cols - WIDTH :])
    wider = lambda rows: jnp.concatenate([pixels[rows], left[rows], right[rows]], axis=1)
    row_edges = edges("row", wider(slice(0, WIDTH)), wider(slice(tile_rows - WIDTH, tile_rows)))
    row_scale = GAUSS[0] / edge_weight(lax.axis_index("row") * tile_rows, tile_rows, rows_total)
    col_scale = 1.0 / edge_weight(lax.axis_index("col") * tile_cols, tile_cols, cols_total)
    col_scale = jnp.broadcast_to(col_scale[:, None], (tile_cols, LANES))
    smoothed, packed = smooth_and_gram(
        pixels, left, right, row_edges, column_taps(tile_cols), row_scale, col_scale
    )
    packed = all_sum(packed)
    mean, projector, scores = components(packed, start, smoothed, float(rows_total * cols_total))
    return (mean, projector, scores)


def solution(mesh):
    in_specs = (P("row", "col", None), P())
    out_specs = (P(), P(), P(None, "row", "col"))
    return jax.shard_map(local, mesh=mesh, in_specs=in_specs, out_specs=out_specs, check_vma=False)
```

```python
import functools

import jax
import jax.numpy as jnp
from jax import lax
from jax.experimental import pallas as pl
from jax.experimental.pallas import tpu as pltpu
from jax.sharding import PartitionSpec as P


ITERS = 4
LANES = 128
AHEAD = 16
CHUNK = 4

GAUSS = (0.0625, 0.25, 0.375, 0.25, 0.0625)


WIDTH = 2
HALO_ROWS = 16


def edges(axis, first, last):
    up = [(i, i + 1) for i in range(lax.axis_size(axis) - 1)]
    down = [(j, i) for i, j in up]
    return lax.ppermute(last, axis, up), lax.ppermute(first, axis, down)


def edge_weight(first, count, total):
    position = first + jnp.arange(count, dtype=jnp.int32)
    weight = jnp.zeros((count,), jnp.float32)
    for offset in range(5):
        inside = (position + offset - 2 >= 0) & (position + offset - 2 < total)
        weight = weight + GAUSS[offset] * inside.astype(jnp.float32)
    return weight


def column_taps(count):
    out = jnp.arange(count, dtype=jnp.int32)[:, None]
    k = jnp.arange(count + HALO_ROWS, dtype=jnp.int32)[None, :]
    beside = k - count
    place = jnp.where(k < count, k, jnp.where(beside < WIDTH, beside - WIDTH, count + beside - WIDTH))
    place = jnp.where(beside < 2 * WIDTH, place, -count)
    taps = jnp.zeros((count, count + HALO_ROWS), jnp.float32)
    for offset in range(5):
        taps = jnp.where(place == out + offset - 2, GAUSS[offset], taps)
    return taps.astype(jnp.bfloat16)


def cascade(c):
    for _ in range(4):
        c = [p + q for p, q in zip(c, c[1:])]
    return c


def correlate(s, gram, ends):
    wide = s.shape[1] - LANES
    over = (((0,), (0,)), ((), ()))
    last = jnp.concatenate([s[:, wide:], jnp.ones((s.shape[0], LANES), jnp.bfloat16)], axis=1)
    gram[...] += lax.dot_general(s[:, :wide], s[:, :wide], over, preferred_element_type=jnp.float32)
    ends[...] += lax.dot_general(s, last, over, preferred_element_type=jnp.float32)


def inner_kernel(
    pixels, left, right, taps, col_scale, smooth_hbm, gram, ends, kept,
    source, across, rounded, smooth, in_sem, out_sem,
):
    tile_rows, tile_cols, feat = pixels.shape
    group = 8
    groups = tile_rows // group
    strip = tile_cols // group
    count = lambda g: group if g + 1 < groups else group - 2 * WIDTH

    def fetch(g):
        rows = pl.ds(g * group, group)
        there = source.at[rows, pl.ds(0, tile_cols), :]
        return pltpu.make_async_copy(pixels.at[rows], there, in_sem.at[g])

    def send(g):
        rows = pl.ds(g * group + WIDTH, count(g))
        return pltpu.make_async_copy(smooth.at[rows], smooth_hbm.at[rows], out_sem.at[g])

    for g in range(groups):
        fetch(g).start()
    source[:, tile_cols:, :] = jnp.zeros((tile_rows, HALO_ROWS, feat), jnp.bfloat16)
    source[:, tile_cols : tile_cols + WIDTH, :] = left[...]
    source[:, tile_cols + WIDTH : tile_cols + 2 * WIDTH, :] = right[...]
    gram[...] = jnp.zeros_like(gram)
    ends[...] = jnp.zeros_like(ends)

    def horizontal(g, q):
        across[g % 4, q] = jnp.dot(taps[...], source[group * g + 4 + q], preferred_element_type=jnp.float32)

    def vertical(g, i):
        at = slice(i * strip, (i + 1) * strip)
        scale = col_scale[at, :] * GAUSS[0]
        for f in range(feat // LANES):
            lanes = slice(f * LANES, (f + 1) * LANES)
            held = []
            for r in range(4 + count(g)):
                v = across[(g - 1) % 4, 4 + r, at, lanes] if r < 4 else across[g % 4, r - 4, at, lanes]
                for k in range(4):
                    if k == len(held):
                        held.append(v)
                        break
                    v, held[k] = v + held[k], v
                else:
                    v = (v * scale).astype(jnp.bfloat16)
                    smooth[g * group + WIDTH + r - 4, at, lanes] = v
                    rounded[g % 2, r - 4, at, lanes] = v

    fetch(0).wait()
    for q in range(4, group):
        horizontal(-1, q)
    fetch(1).wait()
    for q in range(group):
        horizontal(0, q)
    for g in range(groups + 1):
        if g + 2 < groups:
            fetch(g + 2).wait()
        for q in range(group):
            if g + 1 < groups and q < count(g + 1):
                horizontal(g + 1, q)
            if g < groups:
                vertical(g, q)
            if g > 0 and q % CHUNK == CHUNK - 1 and q < count(g - 1):
                rows = rounded[(g - 1) % 2, q - CHUNK + 1 : q + 1]
                correlate(rows.reshape(CHUNK * tile_cols, feat), gram, ends)
        if g < groups:
            send(g).start()
    own = 2 * WIDTH
    kept[:own] = source[:own]
    kept[own:] = source[tile_rows - own :]
    for g in range(groups):
        send(g).wait()


def edge_kernel(
    row_scale, above, below, kept, taps, col_scale, gram_in, ends_in, rounded, packed, beside, across, gram, ends
):
    tile_rows = row_scale.shape[0]
    _, tile_cols, feat = rounded.shape
    own = 2 * WIDTH
    side = own + WIDTH
    beside[:, tile_cols:, :] = jnp.zeros((2 * WIDTH, HALO_ROWS, feat), jnp.bfloat16)
    beside[:WIDTH, 0 : tile_cols + 2 * WIDTH, :] = above[...]
    beside[WIDTH:, 0 : tile_cols + 2 * WIDTH, :] = below[...]
    sources = [beside.at[k] for k in range(WIDTH)] + [kept.at[k] for k in range(2 * own)]
    sources += [beside.at[k] for k in range(WIDTH, 2 * WIDTH)]
    for k, source in enumerate(sources):
        across[k] = jnp.dot(taps[...], source[...], preferred_element_type=jnp.float32)
    strip = 16
    for k, first in enumerate((0, tile_rows - WIDTH)):
        for i in range(tile_cols // strip):
            at = slice(i * strip, (i + 1) * strip)
            scales = [col_scale[at, :] * row_scale[first + r] for r in range(WIDTH)]
            for f in range(feat // LANES):
                lanes = slice(f * LANES, (f + 1) * LANES)
                c = [across[side * k + r, at, lanes] for r in range(side)]
                for r, total in enumerate(cascade(c)):
                    rounded[WIDTH * k + r, at, lanes] = (total * scales[r]).astype(jnp.bfloat16)
    gram[...] = gram_in[...]
    ends[...] = ends_in[...]
    correlate(rounded[...].reshape(2 * WIDTH * tile_cols, feat), gram, ends)
    row = lax.broadcasted_iota(jnp.int32, (LANES, LANES), 0)
    col = lax.broadcasted_iota(jnp.int32, (LANES, LANES), 1)
    n = feat // LANES
    at = 0
    for i in range(n):
        for j in range(i, n):
            rows = slice(i * LANES, (i + 1) * LANES)
            block = ends[rows, :LANES] if j == n - 1 else gram[rows, j * LANES : (j + 1) * LANES]
            if i == j:
                piece = ends[rows, LANES:]
                block = jnp.where((col == 0) & (row > 0), piece, block)
                block = jnp.where((col == 1) & (row == LANES - 1), piece[0:1, :], block)
            packed[at * LANES : (at + 1) * LANES, :] = block
            at += 1


def smooth_and_gram(pixels, left, right, row_edges, taps, row_scale, col_scale):
    tile_rows, tile_cols, feat = pixels.shape
    n = feat // LANES
    wide = feat - LANES
    vmem = pl.BlockSpec(memory_space=pltpu.VMEM)
    hbm = pl.BlockSpec(memory_space=pltpu.HBM)
    smem = pl.BlockSpec(memory_space=pltpu.SMEM)
    pixels = pltpu.with_memory_space_constraint(pixels, pltpu.HBM)
    above, below = row_edges
    width = tile_cols + HALO_ROWS
    smoothed, gram, ends, kept = pl.pallas_call(
        inner_kernel,
        out_shape=(
            pltpu.HBM(pixels.shape, jnp.bfloat16),
            jax.ShapeDtypeStruct((wide, wide), jnp.float32),
            jax.ShapeDtypeStruct((feat, 2 * LANES), jnp.float32),
            jax.ShapeDtypeStruct((4 * WIDTH, width, feat), jnp.bfloat16),
        ),
        in_specs=[hbm, vmem, vmem, vmem, vmem],
        out_specs=(hbm, vmem, vmem, vmem),
        scratch_shapes=[
            pltpu.VMEM((tile_rows, width, feat), jnp.bfloat16),
            pltpu.VMEM((4, 8, tile_cols, feat), jnp.float32),
            pltpu.VMEM((2, 8, tile_cols, feat), jnp.bfloat16),
            pltpu.VMEM(pixels.shape, jnp.bfloat16),
            pltpu.SemaphoreType.DMA((tile_rows // 8,)),
            pltpu.SemaphoreType.DMA((tile_rows // 8,)),
        ],
        compiler_params=pltpu.CompilerParams(vmem_limit_bytes=40 << 20),
        cost_estimate=pl.CostEstimate(flops=10**10, bytes_accessed=3 * 10**7, transcendentals=0),
        name="smooth_inner",
    )(pixels, left, right, taps, col_scale)
    edge_rows, packed = pl.pallas_call(
        edge_kernel,
        out_shape=(
            jax.ShapeDtypeStruct((2 * WIDTH, tile_cols, feat), jnp.bfloat16),
            jax.ShapeDtypeStruct((n * (n + 1) // 2 * LANES, LANES), jnp.float32),
        ),
        in_specs=[smem] + [vmem] * 7,
        out_specs=(vmem, vmem),
        scratch_shapes=[
            pltpu.VMEM((2 * WIDTH, width, feat), jnp.bfloat16),
            pltpu.VMEM((6 * WIDTH, tile_cols, feat), jnp.float32),
            pltpu.VMEM((wide, wide), jnp.float32),
            pltpu.VMEM((feat, 2 * LANES), jnp.float32),
        ],
        compiler_params=pltpu.CompilerParams(vmem_limit_bytes=40 << 20),
        cost_estimate=pl.CostEstimate(flops=10**9, bytes_accessed=10**6, transcendentals=0),
        name="smooth_edges",
    )(row_scale, above, below, kept, taps, col_scale, gram, ends)
    return smoothed, edge_rows, packed


def all_sum(values):
    axes = ("row", "col")
    rows, cols = lax.axis_size("row"), lax.axis_size("col")
    if rows & (rows - 1) or cols & (cols - 1) or cols < 2:
        return lax.psum(values, axes)

    def pairs(row_bit, col_bit):
        return [(r * cols + c, (r ^ row_bit) * cols + (c ^ col_bit)) for r in range(rows) for c in range(cols)]

    core = pairs(0, 1)
    odd = lax.axis_index("col") % 2
    half = values.shape[0] // 2
    mine = lax.dynamic_slice_in_dim(values, odd * half, half)
    other = lax.dynamic_slice_in_dim(values, (1 - odd) * half, half)
    kept = mine + lax.ppermute(other, axes, core)
    row_steps = [pairs(1 << k, 0) for k in range(rows.bit_length() - 1)]
    col_steps = [pairs(0, 1 << k) for k in range(1, cols.bit_length() - 1)]
    order = row_steps[:1] + col_steps + row_steps[1:]
    turned = order[len(order) // 2 :] + order[: len(order) // 2]
    quarter = half // 2
    a, b = kept[:quarter], kept[quarter:]
    for first, second in zip(order, turned):
        got_a = lax.ppermute(a, axes, first)
        got_b = lax.ppermute(b, axes, second)
        a = a + got_a
        b = b + got_b
    kept = jnp.concatenate([a, b])
    got = lax.ppermute(kept, axes, core)
    return jnp.where(odd == 0, jnp.concatenate([kept, got]), jnp.concatenate([got, kept]))


def inverse_factor(a):
    n = a.shape[0]
    row = lax.broadcasted_iota(jnp.int32, (n, n), 0)
    col = lax.broadcasted_iota(jnp.int32, (n, n), 1)
    work = jnp.concatenate([a, (row == col).astype(jnp.float32)], axis=1)
    blocks = [work[8 * i : 8 * i + 8] for i in range(n // 8)]
    sub = lax.broadcasted_iota(jnp.int32, (8, 2 * n), 0)
    ahead = min(AHEAD, n)
    pivots = []
    for j0 in range(0, n, ahead):
        cols = [
            {i: jnp.broadcast_to(blocks[i][:, j : j + 1], (8, 2 * n)) for i in range(j // 8, n // 8)}
            for j in range(j0, j0 + ahead)
        ]
        for k in range(ahead):
            j = j0 + k
            top = j // 8
            s = j - 8 * top
            recip = 1.0 / jnp.broadcast_to(cols[k][top][s : s + 1], (8, 2 * n))
            pivots.append(recip)
            factor = dict(cols[k])
            factor[top] = jnp.where(sub > s, factor[top], 0.0)
            for m in range(k + 1, ahead):
                other = (j0 + m) // 8
                t = j0 + m - 8 * other
                scaled = jnp.broadcast_to(cols[k][other][t : t + 1], (8, 2 * n)) * recip
                for i in cols[m]:
                    cols[m][i] = cols[m][i] - factor[i] * scaled
            line = jnp.broadcast_to(blocks[top][s : s + 1], (8, 2 * n)) * recip
            for i in range(top, n // 8):
                blocks[i] = blocks[i] - factor[i] * line
    out = []
    for i in range(n // 8):
        scale = pivots[8 * i]
        for s in range(1, 8):
            scale = jnp.where(sub == s, pivots[8 * i + s], scale)
        out.append((blocks[i] * lax.sqrt(scale))[:, n:])
    return jnp.concatenate(out, axis=0)


def thirds(x):
    high = x.astype(jnp.bfloat16)
    rest = x - high.astype(jnp.float32)
    middle = rest.astype(jnp.bfloat16)
    return high, middle, (rest - middle.astype(jnp.float32)).astype(jnp.bfloat16)


def dot(a, b, contract):
    return lax.dot_general(a, b, (contract, ((), ())), preferred_element_type=jnp.float32)


def dot_thirds(a, b):
    m = a[0].shape[0]
    one = dot(jnp.concatenate(a, axis=0), b[0], ((1,), (0,)))
    two = dot(jnp.concatenate(a[:2], axis=0), b[1], ((1,), (0,)))
    low = one[2 * m :] + two[m:] + dot(a[0], b[2], ((1,), (0,)))
    return one[:m] + (one[m : 2 * m] + two[:m] + low)


def gram_thirds(y):
    m = y[0].shape[0]
    stack = jnp.concatenate(y, axis=0)
    p = dot(stack, stack, ((1,), (1,)))
    part = lambda i, j: p[i * m : (i + 1) * m, j * m : (j + 1) * m]
    return part(0, 0) + ((part(0, 1) + part(1, 0)) + (part(1, 1) + (part(0, 2) + part(2, 0))))


def components_kernel(
    count, packed, start, edge_rows, smooth_hbm, mean_out, proj_out, scores_hbm,
    cov, cov_thirds, subspace, basis_b, shift, smooth, scores, in_sem, out_sem,
):
    feat = cov.shape[0]
    n = feat // LANES
    rank = start.shape[1]
    tile_rows = smooth.shape[0]
    inner = pl.ds(WIDTH, tile_rows - 2 * WIDTH)
    fetch = pltpu.make_async_copy(smooth_hbm.at[inner], smooth.at[inner], in_sem)
    fetch.start()
    row = lax.broadcasted_iota(jnp.int32, (LANES, LANES), 0)
    col = lax.broadcasted_iota(jnp.int32, (LANES, LANES), 1)
    inv = 1.0 / count
    index = {}
    for i in range(n):
        for j in range(i, n):
            index[i, j] = len(index)
    block = lambda i, j: packed[index[i, j] * LANES : (index[i, j] + 1) * LANES, :]
    means, mean_cols, diag = [], [], []
    for i in range(n):
        b = block(i, i)
        bt = b.T
        first = jnp.broadcast_to(b[LANES - 1 : LANES, 1:2], (LANES, LANES))
        m = jnp.where(row > 0, jnp.broadcast_to(b[:, 0:1], (LANES, LANES)), first) * inv
        means.append(m.T[0:1, :])
        mean_cols.append(m)
        diag.append(jnp.where(row <= col, b, bt))
    mean = jnp.concatenate(means, axis=1)
    mean_out[...] = mean[0]
    for i in range(n):
        for j in range(i, n):
            g = diag[i] if i == j else block(i, j)
            c = g * inv - mean_cols[i] * means[j]
            cov[i * LANES : (i + 1) * LANES, j * LANES : (j + 1) * LANES] = c
            if i != j:
                cov[j * LANES : (j + 1) * LANES, i * LANES : (i + 1) * LANES] = c.T
    split = thirds(cov[...])
    for k in range(3):
        cov_thirds[k] = split[k]
    product = lambda parts: dot_thirds(parts, [cov_thirds[k] for k in range(3)])
    subspace[...] = product(thirds(start[...].T))

    @pl.loop(0, ITERS - 1)
    def _(step):
        parts = thirds(subspace[...])
        z = product(parts)
        lower = inverse_factor(gram_thirds(parts))
        subspace[...] = dot_thirds(thirds(lower), thirds(z))

    parts = thirds(subspace[...])
    lower = inverse_factor(gram_thirds(parts))
    y = dot_thirds(thirds(lower), parts)
    basis = y
    b = thirds(basis)
    left = jnp.concatenate([b[0], b[0], b[1], b[1], b[0], b[2]], axis=0)
    right = jnp.concatenate([b[0], b[1], b[0], b[1], b[2], b[0]], axis=0)
    proj_out[...] = dot(left, right, ((0,), (0,)))
    rounded = basis.astype(jnp.bfloat16)
    basis_b[...] = rounded
    total = jnp.sum(rounded.astype(jnp.float32) * mean, axis=1, keepdims=True)
    shift[...] = jnp.broadcast_to(total, (rank, LANES))
    fetch.wait()
    smooth[:WIDTH] = edge_rows[:WIDTH]
    smooth[tile_rows - WIDTH :] = edge_rows[WIDTH:]

    def send(g):
        here = scores.at[g].reshape(rank, 8, smooth.shape[1])
        return pltpu.make_async_copy(here, scores_hbm.at[:, pl.ds(8 * g, 8), :], out_sem.at[g])

    groups = tile_rows // 8

    @pl.loop(0, groups, unroll=2)
    def _(g):
        for h in range(8):
            s = dot(basis_b[...], smooth[8 * g + h], ((1,), (1,)))
            scores[g, pl.ds(h, rank, stride=8), :] = s - shift[...]
        send(g).start()

    for g in range(groups):
        send(g).wait()


def components(packed, start, edge_rows, smoothed, count):
    tile_rows, tile_cols, feat = smoothed.shape
    rank = start.shape[1]
    vmem = pl.BlockSpec(memory_space=pltpu.VMEM)
    hbm = pl.BlockSpec(memory_space=pltpu.HBM)
    return pl.pallas_call(
        functools.partial(components_kernel, count),
        out_shape=(
            jax.ShapeDtypeStruct((feat,), jnp.float32),
            jax.ShapeDtypeStruct((feat, feat), jnp.float32),
            pltpu.HBM((rank, tile_rows, tile_cols), jnp.float32),
        ),
        in_specs=[vmem, vmem, vmem, hbm],
        out_specs=(vmem, vmem, hbm),
        scratch_shapes=[
            pltpu.VMEM((feat, feat), jnp.float32),
            pltpu.VMEM((3, feat, feat), jnp.bfloat16),
            pltpu.VMEM((rank, feat), jnp.float32),
            pltpu.VMEM((rank, feat), jnp.bfloat16),
            pltpu.VMEM((rank, LANES), jnp.float32),
            pltpu.VMEM((tile_rows, tile_cols, feat), jnp.bfloat16),
            pltpu.VMEM((tile_rows // 8, rank * 8, tile_cols), jnp.float32),
            pltpu.SemaphoreType.DMA,
            pltpu.SemaphoreType.DMA((tile_rows // 8,)),
        ],
        compiler_params=pltpu.CompilerParams(vmem_limit_bytes=40 << 20),
        cost_estimate=pl.CostEstimate(flops=10**9, bytes_accessed=10**7, transcendentals=0),
        name="components",
    )(packed, start, edge_rows, pltpu.with_memory_space_constraint(smoothed, pltpu.HBM))


def local(pixels, start):
    tile_rows, tile_cols, _ = pixels.shape
    rows_total = tile_rows * lax.axis_size("row")
    cols_total = tile_cols * lax.axis_size("col")
    left, right = edges("col", pixels[:, :WIDTH], pixels[:, tile_cols - WIDTH :])
    wider = lambda rows: jnp.concatenate([pixels[rows], left[rows], right[rows]], axis=1)
    row_edges = edges("row", wider(slice(0, WIDTH)), wider(slice(tile_rows - WIDTH, tile_rows)))
    row_scale = GAUSS[0] / edge_weight(lax.axis_index("row") * tile_rows, tile_rows, rows_total)
    col_scale = 1.0 / edge_weight(lax.axis_index("col") * tile_cols, tile_cols, cols_total)
    col_scale = jnp.broadcast_to(col_scale[:, None], (tile_cols, LANES))
    smoothed, edge_rows, packed = smooth_and_gram(
        pixels, left, right, row_edges, column_taps(tile_cols), row_scale, col_scale
    )
    packed = all_sum(packed)
    mean, projector, scores = components(packed, start, edge_rows, smoothed, float(rows_total * cols_total))
    return (mean, projector, scores)


def solution(mesh):
    in_specs = (P("row", "col", None), P())
    out_specs = (P(), P(), P(None, "row", "col"))
    return jax.shard_map(local, mesh=mesh, in_specs=in_specs, out_specs=out_specs, check_vma=False)
```

```python
import functools

import jax
import jax.numpy as jnp
from jax import lax
from jax.experimental import pallas as pl
from jax.experimental.pallas import tpu as pltpu
from jax.sharding import PartitionSpec as P


ITERS = 4
LANES = 128
AHEAD = 16
CHUNK = 4

GAUSS = (0.0625, 0.25, 0.375, 0.25, 0.0625)


WIDTH = 2
HALO_ROWS = 16


def edges(axis, first, last):
    up = [(i, i + 1) for i in range(lax.axis_size(axis) - 1)]
    down = [(j, i) for i, j in up]
    return lax.ppermute(last, axis, up), lax.ppermute(first, axis, down)


def edge_weight(first, count, total):
    position = first + jnp.arange(count, dtype=jnp.int32)
    weight = jnp.zeros((count,), jnp.float32)
    for offset in range(5):
        inside = (position + offset - 2 >= 0) & (position + offset - 2 < total)
        weight = weight + GAUSS[offset] * inside.astype(jnp.float32)
    return weight


def column_taps(count):
    out = jnp.arange(count, dtype=jnp.int32)[:, None]
    k = jnp.arange(count + HALO_ROWS, dtype=jnp.int32)[None, :]
    beside = k - count
    place = jnp.where(k < count, k, jnp.where(beside < WIDTH, beside - WIDTH, count + beside - WIDTH))
    place = jnp.where(beside < 2 * WIDTH, place, -count)
    taps = jnp.zeros((count, count + HALO_ROWS), jnp.float32)
    for offset in range(5):
        taps = jnp.where(place == out + offset - 2, GAUSS[offset], taps)
    return taps.astype(jnp.bfloat16)


def cascade(c):
    for _ in range(4):
        c = [p + q for p, q in zip(c, c[1:])]
    return c


def correlate(s, gram, ends):
    wide = s.shape[1] - LANES
    over = (((0,), (0,)), ((), ()))
    last = jnp.concatenate([s[:, wide:], jnp.ones((s.shape[0], LANES), jnp.bfloat16)], axis=1)
    gram[...] += lax.dot_general(s[:, :wide], s[:, :wide], over, preferred_element_type=jnp.float32)
    ends[...] += lax.dot_general(s, last, over, preferred_element_type=jnp.float32)


def inner_kernel(
    pixels, left, right, taps, col_scale, smooth_hbm, gram, ends, kept,
    source, across, smooth, in_sem, out_sem,
):
    tile_rows, tile_cols, feat = pixels.shape
    group = 8
    groups = tile_rows // group
    strip = tile_cols // group
    count = lambda g: group if g + 1 < groups else group - 2 * WIDTH

    def fetch(g):
        rows = pl.ds(g * group, group)
        there = source.at[rows, pl.ds(0, tile_cols), :]
        return pltpu.make_async_copy(pixels.at[rows], there, in_sem.at[g])

    def send(g):
        rows = pl.ds(g * group + WIDTH, count(g))
        return pltpu.make_async_copy(smooth.at[rows], smooth_hbm.at[rows], out_sem.at[g])

    for g in range(groups):
        fetch(g).start()
    source[:, tile_cols:, :] = jnp.zeros((tile_rows, HALO_ROWS, feat), jnp.bfloat16)
    source[:, tile_cols : tile_cols + WIDTH, :] = left[...]
    source[:, tile_cols + WIDTH : tile_cols + 2 * WIDTH, :] = right[...]
    gram[...] = jnp.zeros_like(gram)
    ends[...] = jnp.zeros_like(ends)

    def horizontal(g, q):
        across[g % 4, q] = jnp.dot(taps[...], source[group * g + 4 + q], preferred_element_type=jnp.float32)

    def vertical(g, i):
        at = slice(i * strip, (i + 1) * strip)
        scale = col_scale[at, :] * GAUSS[0]
        for f in range(feat // LANES):
            lanes = slice(f * LANES, (f + 1) * LANES)
            held = []
            for r in range(4 + count(g)):
                v = across[(g - 1) % 4, 4 + r, at, lanes] if r < 4 else across[g % 4, r - 4, at, lanes]
                for k in range(4):
                    if k == len(held):
                        held.append(v)
                        break
                    v, held[k] = v + held[k], v
                else:
                    v = (v * scale).astype(jnp.bfloat16)
                    smooth[g * group + WIDTH + r - 4, at, lanes] = v

    fetch(0).wait()
    for q in range(4, group):
        horizontal(-1, q)
    fetch(1).wait()
    for q in range(group):
        horizontal(0, q)
    for g in range(groups + 1):
        if g + 2 < groups:
            fetch(g + 2).wait()
        for q in range(group):
            if g + 1 < groups and q < count(g + 1):
                horizontal(g + 1, q)
            if g < groups:
                vertical(g, q)
            if g > 0 and q % CHUNK == CHUNK - 1 and q < count(g - 1):
                first = (g - 1) * group + WIDTH + q - CHUNK + 1
                rows = smooth[first : first + CHUNK]
                correlate(rows.reshape(CHUNK * tile_cols, feat), gram, ends)
        if g < groups:
            send(g).start()
    own = 2 * WIDTH
    kept[:own] = source[:own]
    kept[own:] = source[tile_rows - own :]
    for g in range(groups):
        send(g).wait()


def edge_kernel(
    row_scale, above, below, kept, taps, col_scale, gram_in, ends_in, rounded, packed, beside, across, gram, ends
):
    tile_rows = row_scale.shape[0]
    _, tile_cols, feat = rounded.shape
    own = 2 * WIDTH
    side = own + WIDTH
    beside[:, tile_cols:, :] = jnp.zeros((2 * WIDTH, HALO_ROWS, feat), jnp.bfloat16)
    beside[:WIDTH, 0 : tile_cols + 2 * WIDTH, :] = above[...]
    beside[WIDTH:, 0 : tile_cols + 2 * WIDTH, :] = below[...]
    sources = [beside.at[k] for k in range(WIDTH)] + [kept.at[k] for k in range(2 * own)]
    sources += [beside.at[k] for k in range(WIDTH, 2 * WIDTH)]
    for k, source in enumerate(sources):
        across[k] = jnp.dot(taps[...], source[...], preferred_element_type=jnp.float32)
    strip = 16
    for k, first in enumerate((0, tile_rows - WIDTH)):
        for i in range(tile_cols // strip):
            at = slice(i * strip, (i + 1) * strip)
            scales = [col_scale[at, :] * row_scale[first + r] for r in range(WIDTH)]
            for f in range(feat // LANES):
                lanes = slice(f * LANES, (f + 1) * LANES)
                c = [across[side * k + r, at, lanes] for r in range(side)]
                for r, total in enumerate(cascade(c)):
                    rounded[WIDTH * k + r, at, lanes] = (total * scales[r]).astype(jnp.bfloat16)
    gram[...] = gram_in[...]
    ends[...] = ends_in[...]
    correlate(rounded[...].reshape(2 * WIDTH * tile_cols, feat), gram, ends)
    row = lax.broadcasted_iota(jnp.int32, (LANES, LANES), 0)
    col = lax.broadcasted_iota(jnp.int32, (LANES, LANES), 1)
    n = feat // LANES
    at = 0
    for i in range(n):
        for j in range(i, n):
            rows = slice(i * LANES, (i + 1) * LANES)
            block = ends[rows, :LANES] if j == n - 1 else gram[rows, j * LANES : (j + 1) * LANES]
            if i == j:
                piece = ends[rows, LANES:]
                block = jnp.where((col == 0) & (row > 0), piece, block)
                block = jnp.where((col == 1) & (row == LANES - 1), piece[0:1, :], block)
            packed[at * LANES : (at + 1) * LANES, :] = block
            at += 1


def smooth_and_gram(pixels, left, right, row_edges, taps, row_scale, col_scale):
    tile_rows, tile_cols, feat = pixels.shape
    n = feat // LANES
    wide = feat - LANES
    vmem = pl.BlockSpec(memory_space=pltpu.VMEM)
    hbm = pl.BlockSpec(memory_space=pltpu.HBM)
    smem = pl.BlockSpec(memory_space=pltpu.SMEM)
    pixels = pltpu.with_memory_space_constraint(pixels, pltpu.HBM)
    above, below = row_edges
    width = tile_cols + HALO_ROWS
    smoothed, gram, ends, kept = pl.pallas_call(
        inner_kernel,
        out_shape=(
            pltpu.HBM(pixels.shape, jnp.bfloat16),
            jax.ShapeDtypeStruct((wide, wide), jnp.float32),
            jax.ShapeDtypeStruct((feat, 2 * LANES), jnp.float32),
            jax.ShapeDtypeStruct((4 * WIDTH, width, feat), jnp.bfloat16),
        ),
        in_specs=[hbm, vmem, vmem, vmem, vmem],
        out_specs=(hbm, vmem, vmem, vmem),
        scratch_shapes=[
            pltpu.VMEM((tile_rows, width, feat), jnp.bfloat16),
            pltpu.VMEM((4, 8, tile_cols, feat), jnp.float32),
            pltpu.VMEM(pixels.shape, jnp.bfloat16),
            pltpu.SemaphoreType.DMA((tile_rows // 8,)),
            pltpu.SemaphoreType.DMA((tile_rows // 8,)),
        ],
        compiler_params=pltpu.CompilerParams(vmem_limit_bytes=40 << 20),
        cost_estimate=pl.CostEstimate(flops=10**10, bytes_accessed=3 * 10**7, transcendentals=0),
        name="smooth_inner",
    )(pixels, left, right, taps, col_scale)
    edge_rows, packed = pl.pallas_call(
        edge_kernel,
        out_shape=(
            jax.ShapeDtypeStruct((2 * WIDTH, tile_cols, feat), jnp.bfloat16),
            jax.ShapeDtypeStruct((n * (n + 1) // 2 * LANES, LANES), jnp.float32),
        ),
        in_specs=[smem] + [vmem] * 7,
        out_specs=(vmem, vmem),
        scratch_shapes=[
            pltpu.VMEM((2 * WIDTH, width, feat), jnp.bfloat16),
            pltpu.VMEM((6 * WIDTH, tile_cols, feat), jnp.float32),
            pltpu.VMEM((wide, wide), jnp.float32),
            pltpu.VMEM((feat, 2 * LANES), jnp.float32),
        ],
        compiler_params=pltpu.CompilerParams(vmem_limit_bytes=40 << 20),
        cost_estimate=pl.CostEstimate(flops=10**9, bytes_accessed=10**6, transcendentals=0),
        name="smooth_edges",
    )(row_scale, above, below, kept, taps, col_scale, gram, ends)
    return smoothed, edge_rows, packed


def all_sum(values):
    axes = ("row", "col")
    rows, cols = lax.axis_size("row"), lax.axis_size("col")
    if rows & (rows - 1) or cols & (cols - 1) or cols < 2:
        return lax.psum(values, axes)

    def pairs(row_bit, col_bit):
        return [(r * cols + c, (r ^ row_bit) * cols + (c ^ col_bit)) for r in range(rows) for c in range(cols)]

    core = pairs(0, 1)
    odd = lax.axis_index("col") % 2
    half = values.shape[0] // 2
    mine = lax.dynamic_slice_in_dim(values, odd * half, half)
    other = lax.dynamic_slice_in_dim(values, (1 - odd) * half, half)
    kept = mine + lax.ppermute(other, axes, core)
    row_steps = [pairs(1 << k, 0) for k in range(rows.bit_length() - 1)]
    col_steps = [pairs(0, 1 << k) for k in range(1, cols.bit_length() - 1)]
    order = row_steps[:1] + col_steps + row_steps[1:]
    turned = order[len(order) // 2 :] + order[: len(order) // 2]
    quarter = half // 2
    a, b = kept[:quarter], kept[quarter:]
    for first, second in zip(order, turned):
        got_a = lax.ppermute(a, axes, first)
        got_b = lax.ppermute(b, axes, second)
        a = a + got_a
        b = b + got_b
    kept = jnp.concatenate([a, b])
    got = lax.ppermute(kept, axes, core)
    return jnp.where(odd == 0, jnp.concatenate([kept, got]), jnp.concatenate([got, kept]))


def inverse_factor(a):
    n = a.shape[0]
    row = lax.broadcasted_iota(jnp.int32, (n, n), 0)
    col = lax.broadcasted_iota(jnp.int32, (n, n), 1)
    work = jnp.concatenate([a, (row == col).astype(jnp.float32)], axis=1)
    blocks = [work[8 * i : 8 * i + 8] for i in range(n // 8)]
    sub = lax.broadcasted_iota(jnp.int32, (8, 2 * n), 0)
    ahead = min(AHEAD, n)
    pivots = []
    for j0 in range(0, n, ahead):
        cols = [
            {i: jnp.broadcast_to(blocks[i][:, j : j + 1], (8, 2 * n)) for i in range(j // 8, n // 8)}
            for j in range(j0, j0 + ahead)
        ]
        for k in range(ahead):
            j = j0 + k
            top = j // 8
            s = j - 8 * top
            recip = 1.0 / jnp.broadcast_to(cols[k][top][s : s + 1], (8, 2 * n))
            pivots.append(recip)
            factor = dict(cols[k])
            factor[top] = jnp.where(sub > s, factor[top], 0.0)
            for m in range(k + 1, ahead):
                other = (j0 + m) // 8
                t = j0 + m - 8 * other
                scaled = jnp.broadcast_to(cols[k][other][t : t + 1], (8, 2 * n)) * recip
                for i in cols[m]:
                    cols[m][i] = cols[m][i] - factor[i] * scaled
            line = jnp.broadcast_to(blocks[top][s : s + 1], (8, 2 * n)) * recip
            for i in range(top, n // 8):
                blocks[i] = blocks[i] - factor[i] * line
    out = []
    for i in range(n // 8):
        scale = pivots[8 * i]
        for s in range(1, 8):
            scale = jnp.where(sub == s, pivots[8 * i + s], scale)
        out.append((blocks[i] * lax.sqrt(scale))[:, n:])
    return jnp.concatenate(out, axis=0)


def thirds(x):
    high = x.astype(jnp.bfloat16)
    rest = x - high.astype(jnp.float32)
    middle = rest.astype(jnp.bfloat16)
    return high, middle, (rest - middle.astype(jnp.float32)).astype(jnp.bfloat16)


def dot(a, b, contract):
    return lax.dot_general(a, b, (contract, ((), ())), preferred_element_type=jnp.float32)


def dot_thirds(a, b):
    m = a[0].shape[0]
    one = dot(jnp.concatenate(a, axis=0), b[0], ((1,), (0,)))
    two = dot(jnp.concatenate(a[:2], axis=0), b[1], ((1,), (0,)))
    low = one[2 * m :] + two[m:] + dot(a[0], b[2], ((1,), (0,)))
    return one[:m] + (one[m : 2 * m] + two[:m] + low)


def gram_thirds(y):
    m = y[0].shape[0]
    stack = jnp.concatenate(y, axis=0)
    p = dot(stack, stack, ((1,), (1,)))
    part = lambda i, j: p[i * m : (i + 1) * m, j * m : (j + 1) * m]
    return part(0, 0) + ((part(0, 1) + part(1, 0)) + (part(1, 1) + (part(0, 2) + part(2, 0))))


def components_kernel(
    count, packed, start, edge_rows, smooth_hbm, mean_out, proj_out, scores_hbm,
    cov, cov_thirds, subspace, basis_b, shift, smooth, scores, in_sem, out_sem,
):
    feat = cov.shape[0]
    n = feat // LANES
    rank = start.shape[1]
    tile_rows = smooth.shape[0]
    inner = pl.ds(WIDTH, tile_rows - 2 * WIDTH)
    fetch = pltpu.make_async_copy(smooth_hbm.at[inner], smooth.at[inner], in_sem)
    fetch.start()
    row = lax.broadcasted_iota(jnp.int32, (LANES, LANES), 0)
    col = lax.broadcasted_iota(jnp.int32, (LANES, LANES), 1)
    inv = 1.0 / count
    index = {}
    for i in range(n):
        for j in range(i, n):
            index[i, j] = len(index)
    block = lambda i, j: packed[index[i, j] * LANES : (index[i, j] + 1) * LANES, :]
    means, mean_cols, diag = [], [], []
    for i in range(n):
        b = block(i, i)
        bt = b.T
        first = jnp.broadcast_to(b[LANES - 1 : LANES, 1:2], (LANES, LANES))
        m = jnp.where(row > 0, jnp.broadcast_to(b[:, 0:1], (LANES, LANES)), first) * inv
        means.append(m.T[0:1, :])
        mean_cols.append(m)
        diag.append(jnp.where(row <= col, b, bt))
    mean = jnp.concatenate(means, axis=1)
    mean_out[...] = mean[0]
    for i in range(n):
        for j in range(i, n):
            g = diag[i] if i == j else block(i, j)
            c = g * inv - mean_cols[i] * means[j]
            cov[i * LANES : (i + 1) * LANES, j * LANES : (j + 1) * LANES] = c
            if i != j:
                cov[j * LANES : (j + 1) * LANES, i * LANES : (i + 1) * LANES] = c.T
    split = thirds(cov[...])
    for k in range(3):
        cov_thirds[k] = split[k]
    product = lambda parts: dot_thirds(parts, [cov_thirds[k] for k in range(3)])
    subspace[...] = product(thirds(start[...].T))

    @pl.loop(0, ITERS - 1)
    def _(step):
        parts = thirds(subspace[...])
        z = product(parts)
        lower = inverse_factor(gram_thirds(parts))
        subspace[...] = dot_thirds(thirds(lower), thirds(z))

    parts = thirds(subspace[...])
    lower = inverse_factor(gram_thirds(parts))
    y = dot_thirds(thirds(lower), parts)
    basis = y
    b = thirds(basis)
    left = jnp.concatenate([b[0], b[0], b[1], b[1], b[0], b[2]], axis=0)
    right = jnp.concatenate([b[0], b[1], b[0], b[1], b[2], b[0]], axis=0)
    proj_out[...] = dot(left, right, ((0,), (0,)))
    rounded = basis.astype(jnp.bfloat16)
    basis_b[...] = rounded
    total = jnp.sum(rounded.astype(jnp.float32) * mean, axis=1, keepdims=True)
    shift[...] = jnp.broadcast_to(total, (rank, LANES))
    fetch.wait()
    smooth[:WIDTH] = edge_rows[:WIDTH]
    smooth[tile_rows - WIDTH :] = edge_rows[WIDTH:]

    def send(g):
        here = scores.at[g].reshape(rank, 8, smooth.shape[1])
        return pltpu.make_async_copy(here, scores_hbm.at[:, pl.ds(8 * g, 8), :], out_sem.at[g])

    groups = tile_rows // 8

    @pl.loop(0, groups, unroll=8)
    def _(g):
        for h in range(8):
            s = dot(basis_b[...], smooth[8 * g + h], ((1,), (1,)))
            scores[g, pl.ds(h, rank, stride=8), :] = s - shift[...]
        send(g).start()

    for g in range(groups):
        send(g).wait()


def components(packed, start, edge_rows, smoothed, count):
    tile_rows, tile_cols, feat = smoothed.shape
    rank = start.shape[1]
    vmem = pl.BlockSpec(memory_space=pltpu.VMEM)
    hbm = pl.BlockSpec(memory_space=pltpu.HBM)
    return pl.pallas_call(
        functools.partial(components_kernel, count),
        out_shape=(
            jax.ShapeDtypeStruct((feat,), jnp.float32),
            jax.ShapeDtypeStruct((feat, feat), jnp.float32),
            pltpu.HBM((rank, tile_rows, tile_cols), jnp.float32),
        ),
        in_specs=[vmem, vmem, vmem, hbm],
        out_specs=(vmem, vmem, hbm),
        scratch_shapes=[
            pltpu.VMEM((feat, feat), jnp.float32),
            pltpu.VMEM((3, feat, feat), jnp.bfloat16),
            pltpu.VMEM((rank, feat), jnp.float32),
            pltpu.VMEM((rank, feat), jnp.bfloat16),
            pltpu.VMEM((rank, LANES), jnp.float32),
            pltpu.VMEM((tile_rows, tile_cols, feat), jnp.bfloat16),
            pltpu.VMEM((tile_rows // 8, rank * 8, tile_cols), jnp.float32),
            pltpu.SemaphoreType.DMA,
            pltpu.SemaphoreType.DMA((tile_rows // 8,)),
        ],
        compiler_params=pltpu.CompilerParams(vmem_limit_bytes=40 << 20),
        cost_estimate=pl.CostEstimate(flops=10**9, bytes_accessed=10**7, transcendentals=0),
        name="components",
    )(packed, start, edge_rows, pltpu.with_memory_space_constraint(smoothed, pltpu.HBM))


def local(pixels, start):
    tile_rows, tile_cols, _ = pixels.shape
    rows_total = tile_rows * lax.axis_size("row")
    cols_total = tile_cols * lax.axis_size("col")
    left, right = edges("col", pixels[:, :WIDTH], pixels[:, tile_cols - WIDTH :])
    wider = lambda rows: jnp.concatenate([pixels[rows], left[rows], right[rows]], axis=1)
    row_edges = edges("row", wider(slice(0, WIDTH)), wider(slice(tile_rows - WIDTH, tile_rows)))
    row_scale = GAUSS[0] / edge_weight(lax.axis_index("row") * tile_rows, tile_rows, rows_total)
    col_scale = 1.0 / edge_weight(lax.axis_index("col") * tile_cols, tile_cols, cols_total)
    col_scale = jnp.broadcast_to(col_scale[:, None], (tile_cols, LANES))
    smoothed, edge_rows, packed = smooth_and_gram(
        pixels, left, right, row_edges, column_taps(tile_cols), row_scale, col_scale
    )
    packed = all_sum(packed)
    mean, projector, scores = components(packed, start, edge_rows, smoothed, float(rows_total * cols_total))
    return (mean, projector, scores)


def solution(mesh):
    in_specs = (P("row", "col", None), P())
    out_specs = (P(), P(), P(None, "row", "col"))
    return jax.shard_map(local, mesh=mesh, in_specs=in_specs, out_specs=out_specs, check_vma=False)
```

```python
import functools

import jax
import jax.numpy as jnp
from jax import lax
from jax.experimental import pallas as pl
from jax.experimental.pallas import tpu as pltpu
from jax.sharding import PartitionSpec as P


ITERS = 4
LANES = 128
AHEAD = 16
CHUNK = 4

GAUSS = (0.0625, 0.25, 0.375, 0.25, 0.0625)


WIDTH = 2
HALO_ROWS = 16


def edges(axis, first, last):
    up = [(i, i + 1) for i in range(lax.axis_size(axis) - 1)]
    down = [(j, i) for i, j in up]
    return lax.ppermute(last, axis, up), lax.ppermute(first, axis, down)


def edge_weight(first, count, total):
    position = first + jnp.arange(count, dtype=jnp.int32)
    weight = jnp.zeros((count,), jnp.float32)
    for offset in range(5):
        inside = (position + offset - 2 >= 0) & (position + offset - 2 < total)
        weight = weight + GAUSS[offset] * inside.astype(jnp.float32)
    return weight


def column_taps(count):
    out = jnp.arange(count, dtype=jnp.int32)[:, None]
    k = jnp.arange(count + HALO_ROWS, dtype=jnp.int32)[None, :]
    beside = k - count
    place = jnp.where(k < count, k, jnp.where(beside < WIDTH, beside - WIDTH, count + beside - WIDTH))
    place = jnp.where(beside < 2 * WIDTH, place, -count)
    taps = jnp.zeros((count, count + HALO_ROWS), jnp.float32)
    for offset in range(5):
        taps = jnp.where(place == out + offset - 2, GAUSS[0] * GAUSS[offset], taps)
    return taps.astype(jnp.bfloat16)


def cascade(c):
    for _ in range(4):
        c = [p + q for p, q in zip(c, c[1:])]
    return c


def correlate(s, gram, ends):
    wide = s.shape[1] - LANES
    over = (((0,), (0,)), ((), ()))
    last = jnp.concatenate([s[:, wide:], jnp.ones((s.shape[0], LANES), jnp.bfloat16)], axis=1)
    gram[...] += lax.dot_general(s[:, :wide], s[:, :wide], over, preferred_element_type=jnp.float32)
    ends[...] += lax.dot_general(s, last, over, preferred_element_type=jnp.float32)


def inner_kernel(
    pixels, left, right, taps, col_scale, smooth_hbm, gram, ends, kept,
    source, across, smooth, in_sem, out_sem,
):
    tile_rows, tile_cols, feat = pixels.shape
    group = 8
    groups = tile_rows // group
    strip = tile_cols // group
    count = lambda g: group if g + 1 < groups else group - 2 * WIDTH

    def fetch(g):
        rows = pl.ds(g * group, group)
        there = source.at[rows, pl.ds(0, tile_cols), :]
        return pltpu.make_async_copy(pixels.at[rows], there, in_sem.at[g])

    def send(g):
        rows = pl.ds(g * group + WIDTH, count(g))
        return pltpu.make_async_copy(smooth.at[rows], smooth_hbm.at[rows], out_sem.at[g])

    for g in range(groups):
        fetch(g).start()
    source[:, tile_cols:, :] = jnp.zeros((tile_rows, HALO_ROWS, feat), jnp.bfloat16)
    source[:, tile_cols : tile_cols + WIDTH, :] = left[...]
    source[:, tile_cols + WIDTH : tile_cols + 2 * WIDTH, :] = right[...]
    gram[...] = jnp.zeros_like(gram)
    ends[...] = jnp.zeros_like(ends)

    def horizontal(g, q):
        across[g % 4, q] = jnp.dot(taps[...], source[group * g + 4 + q], preferred_element_type=jnp.float32)

    def vertical(g, i):
        at = slice(i * strip, (i + 1) * strip)
        scale = col_scale[at, :] if i in (0, group - 1) else None
        for f in range(feat // LANES):
            lanes = slice(f * LANES, (f + 1) * LANES)
            held = []
            for r in range(4 + count(g)):
                v = across[(g - 1) % 4, 4 + r, at, lanes] if r < 4 else across[g % 4, r - 4, at, lanes]
                for k in range(4):
                    if k == len(held):
                        held.append(v)
                        break
                    v, held[k] = v + held[k], v
                else:
                    v = (v if scale is None else v * scale).astype(jnp.bfloat16)
                    smooth[g * group + WIDTH + r - 4, at, lanes] = v

    fetch(0).wait()
    for q in range(4, group):
        horizontal(-1, q)
    fetch(1).wait()
    for q in range(group):
        horizontal(0, q)
    for g in range(groups + 1):
        if g + 2 < groups:
            fetch(g + 2).wait()
        for q in range(group):
            if g + 1 < groups and q < count(g + 1):
                horizontal(g + 1, q)
            if g < groups:
                vertical(g, q)
            if g > 0 and q % CHUNK == CHUNK - 1 and q < count(g - 1):
                first = (g - 1) * group + WIDTH + q - CHUNK + 1
                rows = smooth[first : first + CHUNK]
                correlate(rows.reshape(CHUNK * tile_cols, feat), gram, ends)
        if g < groups:
            send(g).start()
    own = 2 * WIDTH
    kept[:own] = source[:own]
    kept[own:] = source[tile_rows - own :]
    for g in range(groups):
        send(g).wait()


def edge_kernel(
    row_scale, above, below, kept, taps, col_scale, gram_in, ends_in, rounded, packed, beside, across, gram, ends
):
    tile_rows = row_scale.shape[0]
    _, tile_cols, feat = rounded.shape
    own = 2 * WIDTH
    side = own + WIDTH
    beside[:, tile_cols:, :] = jnp.zeros((2 * WIDTH, HALO_ROWS, feat), jnp.bfloat16)
    beside[:WIDTH, 0 : tile_cols + 2 * WIDTH, :] = above[...]
    beside[WIDTH:, 0 : tile_cols + 2 * WIDTH, :] = below[...]
    sources = [beside.at[k] for k in range(WIDTH)] + [kept.at[k] for k in range(2 * own)]
    sources += [beside.at[k] for k in range(WIDTH, 2 * WIDTH)]
    for k, source in enumerate(sources):
        across[k] = jnp.dot(taps[...], source[...], preferred_element_type=jnp.float32)
    strip = 16
    for k, first in enumerate((0, tile_rows - WIDTH)):
        for i in range(tile_cols // strip):
            at = slice(i * strip, (i + 1) * strip)
            scales = [col_scale[at, :] * row_scale[first + r] for r in range(WIDTH)]
            for f in range(feat // LANES):
                lanes = slice(f * LANES, (f + 1) * LANES)
                c = [across[side * k + r, at, lanes] for r in range(side)]
                for r, total in enumerate(cascade(c)):
                    rounded[WIDTH * k + r, at, lanes] = (total * scales[r]).astype(jnp.bfloat16)
    gram[...] = gram_in[...]
    ends[...] = ends_in[...]
    correlate(rounded[...].reshape(2 * WIDTH * tile_cols, feat), gram, ends)
    row = lax.broadcasted_iota(jnp.int32, (LANES, LANES), 0)
    col = lax.broadcasted_iota(jnp.int32, (LANES, LANES), 1)
    n = feat // LANES
    at = 0
    for i in range(n):
        for j in range(i, n):
            rows = slice(i * LANES, (i + 1) * LANES)
            block = ends[rows, :LANES] if j == n - 1 else gram[rows, j * LANES : (j + 1) * LANES]
            if i == j:
                piece = ends[rows, LANES:]
                block = jnp.where((col == 0) & (row > 0), piece, block)
                block = jnp.where((col == 1) & (row == LANES - 1), piece[0:1, :], block)
            packed[at * LANES : (at + 1) * LANES, :] = block
            at += 1


def smooth_and_gram(pixels, left, right, row_edges, taps, row_scale, col_scale):
    tile_rows, tile_cols, feat = pixels.shape
    n = feat // LANES
    wide = feat - LANES
    vmem = pl.BlockSpec(memory_space=pltpu.VMEM)
    hbm = pl.BlockSpec(memory_space=pltpu.HBM)
    smem = pl.BlockSpec(memory_space=pltpu.SMEM)
    pixels = pltpu.with_memory_space_constraint(pixels, pltpu.HBM)
    above, below = row_edges
    width = tile_cols + HALO_ROWS
    smoothed, gram, ends, kept = pl.pallas_call(
        inner_kernel,
        out_shape=(
            pltpu.HBM(pixels.shape, jnp.bfloat16),
            jax.ShapeDtypeStruct((wide, wide), jnp.float32),
            jax.ShapeDtypeStruct((feat, 2 * LANES), jnp.float32),
            jax.ShapeDtypeStruct((4 * WIDTH, width, feat), jnp.bfloat16),
        ),
        in_specs=[hbm, vmem, vmem, vmem, vmem],
        out_specs=(hbm, vmem, vmem, vmem),
        scratch_shapes=[
            pltpu.VMEM((tile_rows, width, feat), jnp.bfloat16),
            pltpu.VMEM((4, 8, tile_cols, feat), jnp.float32),
            pltpu.VMEM(pixels.shape, jnp.bfloat16),
            pltpu.SemaphoreType.DMA((tile_rows // 8,)),
            pltpu.SemaphoreType.DMA((tile_rows // 8,)),
        ],
        compiler_params=pltpu.CompilerParams(vmem_limit_bytes=40 << 20),
        cost_estimate=pl.CostEstimate(flops=10**10, bytes_accessed=3 * 10**7, transcendentals=0),
        name="smooth_inner",
    )(pixels, left, right, taps, col_scale)
    edge_rows, packed = pl.pallas_call(
        edge_kernel,
        out_shape=(
            jax.ShapeDtypeStruct((2 * WIDTH, tile_cols, feat), jnp.bfloat16),
            jax.ShapeDtypeStruct((n * (n + 1) // 2 * LANES, LANES), jnp.float32),
        ),
        in_specs=[smem] + [vmem] * 7,
        out_specs=(vmem, vmem),
        scratch_shapes=[
            pltpu.VMEM((2 * WIDTH, width, feat), jnp.bfloat16),
            pltpu.VMEM((6 * WIDTH, tile_cols, feat), jnp.float32),
            pltpu.VMEM((wide, wide), jnp.float32),
            pltpu.VMEM((feat, 2 * LANES), jnp.float32),
        ],
        compiler_params=pltpu.CompilerParams(vmem_limit_bytes=40 << 20),
        cost_estimate=pl.CostEstimate(flops=10**9, bytes_accessed=10**6, transcendentals=0),
        name="smooth_edges",
    )(row_scale, above, below, kept, taps, col_scale, gram, ends)
    return smoothed, edge_rows, packed


def all_sum(values):
    axes = ("row", "col")
    rows, cols = lax.axis_size("row"), lax.axis_size("col")
    if rows & (rows - 1) or cols & (cols - 1) or cols < 2:
        return lax.psum(values, axes)

    def pairs(row_bit, col_bit):
        return [(r * cols + c, (r ^ row_bit) * cols + (c ^ col_bit)) for r in range(rows) for c in range(cols)]

    core = pairs(0, 1)
    odd = lax.axis_index("col") % 2
    half = values.shape[0] // 2
    mine = lax.dynamic_slice_in_dim(values, odd * half, half)
    other = lax.dynamic_slice_in_dim(values, (1 - odd) * half, half)
    kept = mine + lax.ppermute(other, axes, core)
    row_steps = [pairs(1 << k, 0) for k in range(rows.bit_length() - 1)]
    col_steps = [pairs(0, 1 << k) for k in range(1, cols.bit_length() - 1)]
    order = row_steps[:1] + col_steps + row_steps[1:]
    turned = order[len(order) // 2 :] + order[: len(order) // 2]
    quarter = half // 2
    a, b = kept[:quarter], kept[quarter:]
    for first, second in zip(order, turned):
        got_a = lax.ppermute(a, axes, first)
        got_b = lax.ppermute(b, axes, second)
        a = a + got_a
        b = b + got_b
    kept = jnp.concatenate([a, b])
    got = lax.ppermute(kept, axes, core)
    return jnp.where(odd == 0, jnp.concatenate([kept, got]), jnp.concatenate([got, kept]))


def inverse_factor(a):
    n = a.shape[0]
    row = lax.broadcasted_iota(jnp.int32, (n, n), 0)
    col = lax.broadcasted_iota(jnp.int32, (n, n), 1)
    work = jnp.concatenate([a, (row == col).astype(jnp.float32)], axis=1)
    blocks = [work[8 * i : 8 * i + 8] for i in range(n // 8)]
    sub = lax.broadcasted_iota(jnp.int32, (8, 2 * n), 0)
    ahead = min(AHEAD, n)
    pivots = []
    for j0 in range(0, n, ahead):
        cols = [
            {i: jnp.broadcast_to(blocks[i][:, j : j + 1], (8, 2 * n)) for i in range(j // 8, n // 8)}
            for j in range(j0, j0 + ahead)
        ]
        for k in range(ahead):
            j = j0 + k
            top = j // 8
            s = j - 8 * top
            recip = 1.0 / jnp.broadcast_to(cols[k][top][s : s + 1], (8, 2 * n))
            pivots.append(recip)
            factor = dict(cols[k])
            factor[top] = jnp.where(sub > s, factor[top], 0.0)
            for m in range(k + 1, ahead):
                other = (j0 + m) // 8
                t = j0 + m - 8 * other
                scaled = jnp.broadcast_to(cols[k][other][t : t + 1], (8, 2 * n)) * recip
                for i in cols[m]:
                    cols[m][i] = cols[m][i] - factor[i] * scaled
            line = jnp.broadcast_to(blocks[top][s : s + 1], (8, 2 * n)) * recip
            for i in range(top, n // 8):
                blocks[i] = blocks[i] - factor[i] * line
    out = []
    for i in range(n // 8):
        scale = pivots[8 * i]
        for s in range(1, 8):
            scale = jnp.where(sub == s, pivots[8 * i + s], scale)
        out.append((blocks[i] * lax.sqrt(scale))[:, n:])
    return jnp.concatenate(out, axis=0)


def thirds(x):
    high = x.astype(jnp.bfloat16)
    rest = x - high.astype(jnp.float32)
    middle = rest.astype(jnp.bfloat16)
    return high, middle, (rest - middle.astype(jnp.float32)).astype(jnp.bfloat16)


def dot(a, b, contract):
    return lax.dot_general(a, b, (contract, ((), ())), preferred_element_type=jnp.float32)


def dot_thirds(a, b):
    m = a[0].shape[0]
    one = dot(jnp.concatenate(a, axis=0), b[0], ((1,), (0,)))
    two = dot(jnp.concatenate(a[:2], axis=0), b[1], ((1,), (0,)))
    low = one[2 * m :] + two[m:] + dot(a[0], b[2], ((1,), (0,)))
    return one[:m] + (one[m : 2 * m] + two[:m] + low)


def gram_thirds(y):
    m = y[0].shape[0]
    stack = jnp.concatenate(y, axis=0)
    p = dot(stack, stack, ((1,), (1,)))
    part = lambda i, j: p[i * m : (i + 1) * m, j * m : (j + 1) * m]
    return part(0, 0) + ((part(0, 1) + part(1, 0)) + (part(1, 1) + (part(0, 2) + part(2, 0))))


def components_kernel(
    count, packed, start, edge_rows, smooth_hbm, mean_out, proj_out, scores_hbm,
    cov, cov_thirds, subspace, basis_b, shift, smooth, scores, in_sem, out_sem,
):
    feat = cov.shape[0]
    n = feat // LANES
    rank = start.shape[1]
    tile_rows = smooth.shape[0]
    inner = pl.ds(WIDTH, tile_rows - 2 * WIDTH)
    fetch = pltpu.make_async_copy(smooth_hbm.at[inner], smooth.at[inner], in_sem)
    fetch.start()
    row = lax.broadcasted_iota(jnp.int32, (LANES, LANES), 0)
    col = lax.broadcasted_iota(jnp.int32, (LANES, LANES), 1)
    inv = 1.0 / count
    index = {}
    for i in range(n):
        for j in range(i, n):
            index[i, j] = len(index)
    block = lambda i, j: packed[index[i, j] * LANES : (index[i, j] + 1) * LANES, :]
    means, mean_cols, diag = [], [], []
    for i in range(n):
        b = block(i, i)
        bt = b.T
        first = jnp.broadcast_to(b[LANES - 1 : LANES, 1:2], (LANES, LANES))
        m = jnp.where(row > 0, jnp.broadcast_to(b[:, 0:1], (LANES, LANES)), first) * inv
        means.append(m.T[0:1, :])
        mean_cols.append(m)
        diag.append(jnp.where(row <= col, b, bt))
    mean = jnp.concatenate(means, axis=1)
    mean_out[...] = mean[0]
    for i in range(n):
        for j in range(i, n):
            g = diag[i] if i == j else block(i, j)
            c = g * inv - mean_cols[i] * means[j]
            cov[i * LANES : (i + 1) * LANES, j * LANES : (j + 1) * LANES] = c
            if i != j:
                cov[j * LANES : (j + 1) * LANES, i * LANES : (i + 1) * LANES] = c.T
    split = thirds(cov[...])
    for k in range(3):
        cov_thirds[k] = split[k]
    product = lambda parts: dot_thirds(parts, [cov_thirds[k] for k in range(3)])
    subspace[...] = product(thirds(start[...].T))

    @pl.loop(0, ITERS - 1)
    def _(step):
        parts = thirds(subspace[...])
        z = product(parts)
        lower = inverse_factor(gram_thirds(parts))
        subspace[...] = dot_thirds(thirds(lower), thirds(z))

    parts = thirds(subspace[...])
    lower = inverse_factor(gram_thirds(parts))
    y = dot_thirds(thirds(lower), parts)
    basis = y
    b = thirds(basis)
    left = jnp.concatenate([b[0], b[0], b[1], b[1], b[0], b[2]], axis=0)
    right = jnp.concatenate([b[0], b[1], b[0], b[1], b[2], b[0]], axis=0)
    proj_out[...] = dot(left, right, ((0,), (0,)))
    rounded = basis.astype(jnp.bfloat16)
    basis_b[...] = rounded
    total = jnp.sum(rounded.astype(jnp.float32) * mean, axis=1, keepdims=True)
    shift[...] = jnp.broadcast_to(total, (rank, LANES))
    fetch.wait()
    smooth[:WIDTH] = edge_rows[:WIDTH]
    smooth[tile_rows - WIDTH :] = edge_rows[WIDTH:]

    def send(g):
        here = scores.at[g].reshape(rank, 8, smooth.shape[1])
        return pltpu.make_async_copy(here, scores_hbm.at[:, pl.ds(8 * g, 8), :], out_sem.at[g])

    groups = tile_rows // 8

    @pl.loop(0, groups, unroll=8)
    def _(g):
        for h in range(8):
            s = dot(basis_b[...], smooth[8 * g + h], ((1,), (1,)))
            scores[g, pl.ds(h, rank, stride=8), :] = s - shift[...]
        send(g).start()

    for g in range(groups):
        send(g).wait()


def components(packed, start, edge_rows, smoothed, count):
    tile_rows, tile_cols, feat = smoothed.shape
    rank = start.shape[1]
    vmem = pl.BlockSpec(memory_space=pltpu.VMEM)
    hbm = pl.BlockSpec(memory_space=pltpu.HBM)
    return pl.pallas_call(
        functools.partial(components_kernel, count),
        out_shape=(
            jax.ShapeDtypeStruct((feat,), jnp.float32),
            jax.ShapeDtypeStruct((feat, feat), jnp.float32),
            pltpu.HBM((rank, tile_rows, tile_cols), jnp.float32),
        ),
        in_specs=[vmem, vmem, vmem, hbm],
        out_specs=(vmem, vmem, hbm),
        scratch_shapes=[
            pltpu.VMEM((feat, feat), jnp.float32),
            pltpu.VMEM((3, feat, feat), jnp.bfloat16),
            pltpu.VMEM((rank, feat), jnp.float32),
            pltpu.VMEM((rank, feat), jnp.bfloat16),
            pltpu.VMEM((rank, LANES), jnp.float32),
            pltpu.VMEM((tile_rows, tile_cols, feat), jnp.bfloat16),
            pltpu.VMEM((tile_rows // 8, rank * 8, tile_cols), jnp.float32),
            pltpu.SemaphoreType.DMA,
            pltpu.SemaphoreType.DMA((tile_rows // 8,)),
        ],
        compiler_params=pltpu.CompilerParams(vmem_limit_bytes=40 << 20),
        cost_estimate=pl.CostEstimate(flops=10**9, bytes_accessed=10**7, transcendentals=0),
        name="components",
    )(packed, start, edge_rows, pltpu.with_memory_space_constraint(smoothed, pltpu.HBM))


def local(pixels, start):
    tile_rows, tile_cols, _ = pixels.shape
    rows_total = tile_rows * lax.axis_size("row")
    cols_total = tile_cols * lax.axis_size("col")
    left, right = edges("col", pixels[:, :WIDTH], pixels[:, tile_cols - WIDTH :])
    wider = lambda rows: jnp.concatenate([pixels[rows], left[rows], right[rows]], axis=1)
    row_edges = edges("row", wider(slice(0, WIDTH)), wider(slice(tile_rows - WIDTH, tile_rows)))
    row_scale = 1.0 / edge_weight(lax.axis_index("row") * tile_rows, tile_rows, rows_total)
    col_scale = 1.0 / edge_weight(lax.axis_index("col") * tile_cols, tile_cols, cols_total)
    col_scale = jnp.broadcast_to(col_scale[:, None], (tile_cols, LANES))
    smoothed, edge_rows, packed = smooth_and_gram(
        pixels, left, right, row_edges, column_taps(tile_cols), row_scale, col_scale
    )
    packed = all_sum(packed)
    mean, projector, scores = components(packed, start, edge_rows, smoothed, float(rows_total * cols_total))
    return (mean, projector, scores)


def solution(mesh):
    in_specs = (P("row", "col", None), P())
    out_specs = (P(), P(), P(None, "row", "col"))
    return jax.shard_map(local, mesh=mesh, in_specs=in_specs, out_specs=out_specs, check_vma=False)
```
